256 devices in a mesh: gx: 4 (over z_hi), gy: 4 (over z_lo, core), gz: 16 (over y, x).
Axes of the slice: x: 4, y: 4, z: 8 (z_hi: 4, z_lo: 2; z = z_hi * 2 + z_lo), core: 2. Of those that a mesh axis runs over, the one named last changes fastest.
Arguments:
- populations: float32 [19, 128, 128, 512], P(None, 'gz', 'gy', 'gx'), as said below
- rbf_weights: bfloat16 [16384, 128, 128], P(('gx', 'gy', 'gz')), may hold values from -0.5 to 0.5
- owner_map: int32 [16384, 1], P(('gx', 'gy', 'gz')), may hold values from 0 to 63; in each aligned block of 64 rows (0 to 63, 64 to 127, ...) at most 2 rows name the same one
- shell_slot: int32 [16384, 1], P(('gx', 'gy', 'gz')), may hold values from 0 to 7
- compliance: float32 [2048, 128, 128], P(('gx', 'gy', 'gz')), may hold values from -0.5 to 0.5
- neighbour_compliance: float32 [32768, 128], P(('gx', 'gy', 'gz')), may hold values from -0.5 to 0.5
- interface_row: int32 [16384], P(('gx', 'gy', 'gz')), may hold values from 0 to 255, as said below
Outputs:
- new_populations: float32 [19, 128, 128, 512], P(None, 'gz', 'gy', 'gx')
- displacement: float32 [2048, 3, 128], P(('gx', 'gy', 'gz'))
- wall_motion: float32 [16384, 3, 128], P(('gx', 'gy', 'gz'))
The draws below stay inside these ranges and needn't reach their ends.
Inputs may be any that keep to these rules, and one draw needn't show every extreme that they name: `populations`: each population lies between 0.5 and 1.5 times its lattice weight. `owner_map`: among the 64 rows of one device no owner appears more than 2 times, and some owner appears exactly 2 times. `interface_row`: the 64 rows of one device are distinct.
All inputs are finite; a program needn't handle non-finite values.
Results may differ from the reference program's by a relative error of at most 0.004.
Values sent between devices are 32-bit elements; how exact they have to be, the bound alone decides.
No kernel may reach another device: no remote copies, remote signals or barrier semaphores. Data moves between devices by JAX's collectives and lax.ppermute only.
A program may use at most 64 MiB of HBM per device.

```python
import math
import jax
import jax.numpy as jnp
import numpy as np
from jax import lax

CX = 128
CY = 32
CZ = 8
NB = 64
SB = 8
SN = 128
CAP = 2
NX = 512
NY = 128
NZ = 128
INTERFACE = 16384
SHELL_BLOCKS = 2048
N_GX = 4
N_GY = 4
N_GZ = 16
DEVICES = 256


lattice_weight = (1.0 / 3.0,) + (1.0 / 18.0,) * 6 + (1.0 / 36.0,) * 12


def draw_populations(key, part):
    weights = jnp.array(lattice_weight, dtype=jnp.float32)
    factor = jax.random.uniform(key, (19, NZ, NY, NX), jnp.float32, 0.5, 1.5)
    return weights[:, None, None, None] * factor


def pick_rows(device_key):
    return jax.random.permutation(device_key, CZ * CY)[:NB]


def draw_interface_row(key, part):
    device_keys = jax.random.split(jax.random.fold_in(key, 23), INTERFACE // NB)
    chosen = jax.vmap(pick_rows)(device_keys)
    return chosen.reshape(INTERFACE).astype(jnp.int32)


def plant(result, key, low, high):
    place = [jax.random.randint(jax.random.fold_in(key, axis), (), 0, length) for axis, length in enumerate(result.shape)]
    widest = result.shape.index(max(result.shape))
    beside = place[:widest] + [(place[widest] + 1) % result.shape[widest]] + place[widest + 1:]
    return result.at[tuple(place)].set(low).at[tuple(beside)].set(high)


def levels(own_key, dims, cuts, smallest, high):
    def one(dim, shards_of):
        heights = jax.random.uniform(jax.random.fold_in(jax.random.fold_in(own_key, 6), dim), (shards_of,), jnp.float32, smallest / len(cuts), high / len(cuts))
        return jnp.repeat(jnp.exp(heights), dims[dim] // shards_of).reshape((-1,) + (1,) * (len(dims) - dim - 1))

    level = one(*cuts[0])
    for cut in cuts[1:]:
        level = level * one(*cut)
    return level


def routed_block(key, own, number, rows, count, top, limit, skew):
    ranking = jax.random.permutation(key, count)
    heavy_load, ordinary = load_shares(count, rows * top, limit, skew, True), load_shares(count, rows * top, limit, skew, False)
    places = jnp.arange(count)

    def named(sizes, offset_by):
        used = int((sizes > 0).sum())
        fixed = max(1, used // 4)
        moved = fixed + (places - fixed + offset_by * (used - fixed)) % max(1, count - fixed)
        return jnp.zeros((count,), jnp.int32).at[ranking[jnp.where(places < fixed, places, moved)]].set(jnp.asarray(sizes, jnp.int32))

    sizes = jnp.where(number % 4 == 0, named(heavy_load, number // 4), named(ordinary, number - number // 4 - 1))
    mixed = jax.random.permutation(jax.random.fold_in(own, 3), count)
    source_of, receiver = mixed[0:count // 2 * 2:2], mixed[1:count // 2 * 2:2]
    room = jnp.minimum(sizes[source_of] - 1, limit - sizes[receiver]) // 2
    room = jnp.where((source_of == ranking[0]) | (receiver == ranking[0]) | (sizes[receiver] == 0), 0, jnp.maximum(room, 0))
    moved = jax.random.randint(jax.random.fold_in(own, 4), (count // 2,), 0, 1 << 20) % (room + 1)
    sizes = sizes.at[source_of].add(-moved).at[receiver].add(moved)
    labels = jnp.searchsorted(jnp.cumsum(sizes), jnp.arange(rows * top), side="right").astype(jnp.int32)
    table = labels.reshape(top, rows).T
    table = table[jax.random.permutation(jax.random.fold_in(own, 1), rows)]
    offset_by = jax.random.randint(jax.random.fold_in(own, 2), (rows, 1), 0, top)
    return jnp.take_along_axis(table, (jnp.arange(top)[None, :] + offset_by) % top, axis=1)


def load_shares(count, total, limit, lean, full):
    portions = [(1 << 20) // math.isqrt(standing ** lean) + 1 for standing in range(1, count + 1)]
    largest = limit if full else min(limit, max(-(-total // count), total * portions[0] // sum(portions)))
    least = 1 if total - largest >= count - 1 else 0
    counts, rest = [largest] + [least] * (count - 1), total - largest - least * (count - 1)
    while rest > 0:
        free = [i for i in range(1, count) if counts[i] < largest] or [i for i in range(1, count) if counts[i] < limit]
        whole, budget = sum([portions[i] for i in free]), rest
        for i in free:
            more = min(limit - counts[i], max(1, budget * portions[i] // whole), rest)
            counts[i] = counts[i] + more
            rest = rest - more
    return np.array(counts)


def bell_draw(key, shape, deviation, bound, cuts=(), held_as=jnp.bfloat16):
    result = deviation * jax.random.normal(key, shape, jnp.float32)
    if cuts:
        result = result * levels(key, shape, cuts, -0.22, 0.18)
    return jnp.clip(result, -bound, bound).astype(held_as)


def setup_inputs(seed: int = 0) -> dict:
    streams_of = jax.random.split(jax.random.key(seed), 8)
    populations = draw_populations(jax.random.fold_in(streams_of[7], 71), 0)
    rbf_weights = bell_draw(streams_of[1], (INTERFACE, CX, SN), CX ** -0.5, 0.5, ((0, 256),))
    owner_map_keys = jax.random.split(jax.random.fold_in(streams_of[2], 1), INTERFACE // NB)
    owner_map_turns = jax.random.permutation(jax.random.fold_in(streams_of[2], 3), INTERFACE // NB)
    owner_map = jax.vmap(lambda own, number: routed_block(jax.random.fold_in(streams_of[2], 2), own, number, NB, N_GY * N_GZ, 1, CAP, 2))(owner_map_keys, owner_map_turns).reshape((INTERFACE, 1))
    shell_slot = plant(jax.random.randint(streams_of[3], (INTERFACE, 1), 0, SB), jax.random.fold_in(streams_of[3], 1), 0, SB - 1).astype(jnp.int32)
    compliance = bell_draw(streams_of[4], (SHELL_BLOCKS, SN, SN), SN ** -0.5, 0.5, ((0, 256),), jnp.float32)
    neighbour_compliance = bell_draw(streams_of[5], (DEVICES * SN, SN), SN ** -0.5, 0.5, ((0, 256),), jnp.float32)
    interface_row = draw_interface_row(jax.random.fold_in(streams_of[7], 71), 0)
    return {"populations": populations, "rbf_weights": rbf_weights, "owner_map": owner_map, "shell_slot": shell_slot, "compliance": compliance, "neighbour_compliance": neighbour_compliance, "interface_row": interface_row}


lattice_velocity = ((0, 0, 0), (1, 0, 0), (-1, 0, 0), (0, 1, 0), (0, -1, 0), (0, 0, 1), (0, 0, -1),
                    (1, 1, 0), (-1, -1, 0), (1, -1, 0), (-1, 1, 0), (1, 0, 1), (-1, 0, -1), (1, 0, -1),
                    (-1, 0, 1), (0, 1, 1), (0, -1, -1), (0, 1, -1), (0, -1, 1))
lattice_weight = (1.0 / 3.0,) + (1.0 / 18.0,) * 6 + (1.0 / 36.0,) * 12
load_scale = 30.0
relaxation = 1.6


def moment_matrix():
    return jnp.array([[1.0] * 19,
                      [float(item[0]) for item in lattice_velocity],
                      [float(item[1]) for item in lattice_velocity],
                      [float(item[2]) for item in lattice_velocity]], dtype=jnp.float32)


def collide(flattened):
    moments = jnp.dot(moment_matrix(), flattened, precision=lax.Precision.HIGHEST)
    density = moments[0]
    velocity = moments[1:4] / density
    speed_square = velocity[0] * velocity[0] + velocity[1] * velocity[1] + velocity[2] * velocity[2]
    relaxed = []
    for direction in range(19):
        along_x, along_y, along_z = lattice_velocity[direction]
        projected = along_x * velocity[0] + along_y * velocity[1] + along_z * velocity[2]
        equilibrium = lattice_weight[direction] * density * (
            1.0 + 3.0 * projected + 4.5 * projected * projected - 1.5 * speed_square)
        relaxed.append(flattened[direction] - relaxation * (flattened[direction] - equilibrium))
    return relaxed, moments


def block_forces(pair):
    traction, weights = pair
    return jnp.einsum('bkc,bcs->bks', traction.astype(jnp.float32), weights.astype(jnp.float32),
                      precision=lax.Precision.HIGHEST)


def block_motion(pair):
    returned, weights = pair
    return jnp.einsum('bks,bcs->bkc', returned.astype(jnp.float32), weights.astype(jnp.float32),
                      precision=lax.Precision.HIGHEST)


def reference(populations, rbf_weights, owner_map, shell_slot, compliance, neighbour_compliance, interface_row):
    grid_shape = populations.shape[1:]
    relaxed, moments = collide(populations.reshape(19, -1))
    passed = []
    for direction in range(19):
        along_x, along_y, along_z = lattice_velocity[direction]
        passed.append(jnp.roll(relaxed[direction].reshape(grid_shape), (along_z, along_y, along_x), axis=(0, 1, 2)))
    new_populations = jnp.stack(passed)

    owner_count = N_GY * N_GZ
    devices = INTERFACE // NB
    device_index = jnp.arange(INTERFACE, dtype=jnp.int32) // NB
    slab_index = device_index // owner_count
    pencil_index = (device_index // N_GZ) % N_GY
    block_index = device_index % N_GZ
    cell_z = block_index * CZ + interface_row // CY
    cell_y = pencil_index * CY + interface_row % CY
    momentum = moments[1:4].reshape(3, NZ, NY, N_GX, CX)
    interface_momentum = jnp.transpose(momentum[:, cell_z, cell_y, slab_index, :], (1, 0, 2))
    traction = (load_scale * interface_momentum).astype(jnp.bfloat16)
    forces = lax.map(block_forces, (traction.reshape(devices, NB, 3, CX),
                                    rbf_weights.reshape(devices, NB, CX, SN)))
    forces = forces.reshape(INTERFACE, 3 * SN)

    target = ((slab_index * owner_count + owner_map[:, 0]) * SB + shell_slot[:, 0]).astype(jnp.int32)
    loads = jax.ops.segment_sum(forces, target, num_segments=SHELL_BLOCKS).reshape(SHELL_BLOCKS, 3, SN)
    displacement = jnp.einsum('skn,snm->skm', loads, compliance, precision=lax.Precision.HIGHEST)
    last_loads = loads.reshape(devices, SB, 3, SN)[:, SB - 1]
    previous = jnp.concatenate([jnp.zeros((1, 3, SN), jnp.float32), last_loads[:-1]], 0)
    has_left = (jnp.arange(devices, dtype=jnp.int32) % owner_count > 0).astype(jnp.float32)
    shared_term = jnp.einsum('dkn,dnm->dkm', previous, neighbour_compliance.reshape(devices, SN, SN),
                             precision=lax.Precision.HIGHEST) * has_left[:, None, None]
    displacement = displacement.reshape(devices, SB, 3, SN).at[:, 0].add(shared_term).reshape(SHELL_BLOCKS, 3, SN)

    returned = displacement[target].astype(jnp.bfloat16)
    wall_motion = lax.map(block_motion, (returned.reshape(devices, NB, 3, SN),
                                         rbf_weights.reshape(devices, NB, CX, SN)))
    return new_populations, displacement, wall_motion.reshape(INTERFACE, 3, CX)
```

```python
import jax
import jax.numpy as jnp
from jax import lax
from jax.experimental import pallas as pl
from jax.experimental.pallas import tpu as pltpu
from jax.sharding import PartitionSpec as P


lattice_velocity = (
    (0, 0, 0),
    (1, 0, 0),
    (-1, 0, 0),
    (0, 1, 0),
    (0, -1, 0),
    (0, 0, 1),
    (0, 0, -1),
    (1, 1, 0),
    (-1, -1, 0),
    (1, -1, 0),
    (-1, 1, 0),
    (1, 0, 1),
    (-1, 0, -1),
    (1, 0, -1),
    (-1, 0, 1),
    (0, 1, 1),
    (0, -1, -1),
    (0, 1, -1),
    (0, -1, 1),
)
lattice_weight = (1.0 / 3.0,) + (1.0 / 18.0,) * 6 + (1.0 / 36.0,) * 12
load_scale = 30.0
relaxation = 1.6

CZ, CY, CX = 8, 32, 128
ROWS = CZ * CY
NB, SB, SN = 64, 8, 128
OWNERS = 64
NEAR_BLOCKS = 16
OUT_ROWS = 10
BACK_ROWS = 7

VMEM = pl.BlockSpec(memory_space=pltpu.VMEM)
SMEM = pl.BlockSpec(memory_space=pltpu.SMEM)
ANY = pl.BlockSpec(memory_space=pl.ANY)


def moved(component, sign):
    return [d for d in range(19) if lattice_velocity[d][component] == sign]


XP, XM = moved(0, 1), moved(0, -1)
YP, YM = moved(1, 1), moved(1, -1)
ZP, ZM = moved(2, 1), moved(2, -1)
MOVING = XP + XM
STILL = moved(0, 0)
TURNED = [d for d in STILL if lattice_velocity[d][1] != 0]
BENT = [d for d in MOVING if lattice_velocity[d][1] != 0]
DIAGONAL = [d for d in TURNED if lattice_velocity[d][2] != 0]


def signed_sum(values, component):
    total = None
    for d in range(19):
        c = lattice_velocity[d][component]
        if c == 0:
            continue
        if total is None:
            total = values[d]
        elif c > 0:
            total = total + values[d]
        else:
            total = total - values[d]
    return total


def shape(dims, dtype=jnp.float32):
    return jax.ShapeDtypeStruct(dims, dtype)


def near(dims):
    return pltpu.VMEM(dims, jnp.float32)


def held(value):
    return pltpu.with_memory_space_constraint(value, pltpu.VMEM)


def far(value):
    return pltpu.with_memory_space_constraint(value, pltpu.HBM)


def cost(flops, moved_bytes):
    return pl.CostEstimate(flops=flops, bytes_accessed=moved_bytes, transcendentals=0)


def forces_body(
    row_hbm, owner_hbm, slot_hbm, pop_hbm, w_hbm, out_ref,
    row_s, owner_s, slot_s, pop, w, mom, seen, pop_sem, w_sem, in_sem,
):
    parts = 4
    integers = [
        pltpu.make_async_copy(a, b, in_sem.at[i])
        for i, (a, b) in enumerate(((row_hbm, row_s), (owner_hbm, owner_s), (slot_hbm, slot_s)))
    ]
    pop_copies = []
    for c in range(parts):
        rows = pl.ds(c * (ROWS // parts), ROWS // parts)
        pop_copies.append(
            pltpu.make_async_copy(pop_hbm.at[:, rows], pop.at[:, rows], pop_sem.at[c])
        )
    w_copies = []
    for c in range(parts):
        blocks = pl.ds(c * (NB // parts), NB // parts)
        w_copies.append(pltpu.make_async_copy(w_hbm.at[blocks], w.at[blocks], w_sem.at[c]))
    for copy in pop_copies + integers + w_copies:
        copy.start()
    out_ref[...] = jnp.zeros(out_ref.shape, jnp.float32)
    for o in range(OWNERS):
        seen[o] = 0
    for c in range(parts):
        pop_copies[c].wait()
        for t in range(c * (ROWS // parts // 8), (c + 1) * (ROWS // parts // 8)):
            values = [pop[d, t * 8 : t * 8 + 8, :] for d in range(19)]
            for k in range(3):
                mom[pl.ds(t * 64 + k, 8, stride=8), :] = load_scale * signed_sum(values, k)
    lane = lax.broadcasted_iota(jnp.int32, (1, 128), 1)
    for copy in integers:
        copy.wait()
    for b in range(NB):
        if b % (NB // parts) == 0:
            w_copies[b // (NB // parts)].wait()
        traction = mom[pl.ds(pl.multiple_of(row_s[b] * 8, 8), 8), :].astype(jnp.bfloat16)
        force = jnp.dot(traction, w[b], preferred_element_type=jnp.float32)[:3]
        owner = owner_s[b]
        rank = seen[owner]
        seen[owner] = rank + 1
        slot = slot_s[b]
        start = owner * OUT_ROWS
        out_ref[pl.ds(start + rank * 3, 3), :] = force
        pltpu.store(
            out_ref.at[pl.ds(start + 9, 1), :],
            jnp.full((1, 128), (slot + 1).astype(jnp.float32)),
            mask=lane == rank,
        )
        shared = jnp.logical_and(slot == SB - 1, owner < OWNERS - 1)
        after = jnp.where(owner < OWNERS - 1, owner + 1, 0) * OUT_ROWS + 6
        out_ref[pl.ds(after, 3), :] += jnp.where(shared, force, 0.0)


def send_forces(rows, owners, slots, populations, weights):
    return pl.pallas_call(
        forces_body,
        out_shape=near((OWNERS * OUT_ROWS, 128)),
        in_specs=[ANY] * 5,
        out_specs=VMEM,
        scratch_shapes=[
            pltpu.SMEM((NB,), jnp.int32),
            pltpu.SMEM((NB,), jnp.int32),
            pltpu.SMEM((NB,), jnp.int32),
            pltpu.VMEM((19, ROWS, CX), jnp.float32),
            pltpu.VMEM((NB, CX, SN), jnp.bfloat16),
            pltpu.VMEM((ROWS * 8, CX), jnp.float32),
            pltpu.SMEM((OWNERS,), jnp.int32),
            pltpu.SemaphoreType.DMA((4,)),
            pltpu.SemaphoreType.DMA((4,)),
            pltpu.SemaphoreType.DMA((3,)),
        ],
        cost_estimate=cost(50_000_000, 5_000_000),
        compiler_params=pltpu.CompilerParams(vmem_limit_bytes=16 * 1024 * 1024),
        name="forces",
    )(far(rows), far(owners), far(slots), far(populations), far(weights))


def two_parts(x):
    high = x.astype(jnp.bfloat16)
    return high, (x - high.astype(jnp.float32)).astype(jnp.bfloat16)


def owner_body(in_ref, comp_hbm, near_hbm, yz_ref, disp_ref, back_ref, comp, left, right, sem):
    copies = [pltpu.make_async_copy(near_hbm, comp.at[SB], sem.at[SB])]
    for s in range(SB):
        copies.append(pltpu.make_async_copy(comp_hbm.at[s], comp.at[s], sem.at[s]))
    for copy in copies:
        copy.start()

    b, e = lax.axis_index("gy"), lax.axis_index("gz")
    for j, d in enumerate(DIAGONAL):
        _, cy, cz = lattice_velocity[d]
        chunk = lax.rem(b + cy + 4, 4) * 16 + lax.rem(e + cz + 16, 16)
        back_ref[pl.ds(chunk * BACK_ROWS + 6, 1), :] = yz_ref[j : j + 1, :]

    def rows_of(j):
        return in_ref[pl.ds(j, OWNERS, stride=OUT_ROWS), :]

    def mm(a, b):
        return jnp.dot(a, b, preferred_element_type=jnp.float32)

    tags = rows_of(9)
    lane = lax.broadcasted_iota(jnp.int32, (OWNERS, 128), 1).astype(jnp.float32) + 1.0
    chosen = jnp.concatenate(
        [
            (jnp.broadcast_to(tags[:, r : r + 1], (OWNERS, 128)) == lane).astype(jnp.float32)
            for r in range(2)
        ],
        axis=0,
    )
    select = chosen.T[:SB].astype(jnp.bfloat16)
    left[...] = jnp.zeros(left.shape, jnp.float32)
    for k in range(3):
        arrived = jnp.concatenate([rows_of(k), rows_of(3 + k)], axis=0)
        high, low = two_parts(arrived)
        loads = mm(select, high) + mm(select, low)
        high, low = two_parts(loads)
        left[pl.ds(k, SB, stride=8), :] = high.astype(jnp.float32)
        left[pl.ds(3 + k, SB, stride=8), :] = low.astype(jnp.float32)
        shared = jnp.sum(rows_of(6 + k), axis=0, keepdims=True)
        high, low = two_parts(shared)
        left[SB * 8 + k : SB * 8 + k + 1, :] = high.astype(jnp.float32)
        left[SB * 8 + 3 + k : SB * 8 + 4 + k, :] = low.astype(jnp.float32)

    def product(s, matrix):
        high, low = two_parts(matrix)
        rows = left[s * 8 : s * 8 + 8, :].astype(jnp.bfloat16)
        first = mm(rows, high)
        return first[:3] + first[3:6] + mm(rows, low)[:3]

    copies[0].wait()
    for s in range(SB):
        copies[1 + s].wait()
        moved_by = product(s, comp[s])
        if s == 0:
            moved_by = moved_by + product(SB, comp[SB])
        disp_ref[:, s, :] = moved_by
        right[s * 8 : s * 8 + 3, :] = moved_by
    chosen = chosen.astype(jnp.bfloat16)
    for k in range(3):
        nodes = right[pl.ds(k, SB, stride=8), :].astype(jnp.bfloat16).astype(jnp.float32)
        nodes = jnp.concatenate([nodes, jnp.zeros((128 - SB, 128), jnp.float32)], axis=0)
        back = mm(chosen, nodes.astype(jnp.bfloat16))
        for r in range(2):
            back_ref[pl.ds(3 * r + k, OWNERS, stride=BACK_ROWS), :] = back[
                r * OWNERS : (r + 1) * OWNERS
            ]


def owner_step(arrived, compliance, neighbour, lines):
    return pl.pallas_call(
        owner_body,
        out_shape=(shape((3, SB, SN)), near((OWNERS * BACK_ROWS, 128))),
        in_specs=[VMEM, ANY, ANY, VMEM],
        out_specs=(VMEM, VMEM),
        scratch_shapes=[
            pltpu.VMEM((SB + 1, SN, SN), jnp.float32),
            pltpu.VMEM((SB * 8 + 8, 128), jnp.float32),
            pltpu.VMEM((SB * 8, 128), jnp.float32),
            pltpu.SemaphoreType.DMA((SB + 1,)),
        ],
        cost_estimate=cost(20_000_000, 1_200_000),
        compiler_params=pltpu.CompilerParams(vmem_limit_bytes=16 * 1024 * 1024),
        name="owner",
    )(held(arrived), far(compliance), far(neighbour), held(lines))


def wall_body(owner_hbm, in_ref, w_near, w_hbm, out_ref, owner_s, w, seen, w_sem, in_sem):
    owner_copy = pltpu.make_async_copy(owner_hbm, owner_s, in_sem)
    owner_copy.start()
    parts = 6
    size = (NB - NEAR_BLOCKS) // parts
    w_copies = []
    for c in range(parts):
        w_copies.append(
            pltpu.make_async_copy(
                w_hbm.at[pl.ds(NEAR_BLOCKS + c * size, size)], w.at[pl.ds(c * size, size)], w_sem.at[c]
            )
        )
    for copy in w_copies:
        copy.start()
    for o in range(OWNERS):
        seen[o] = 0
    owner_copy.wait()
    for b in range(NB):
        if b < NEAR_BLOCKS:
            weight = w_near[b]
        else:
            if (b - NEAR_BLOCKS) % size == 0:
                w_copies[(b - NEAR_BLOCKS) // size].wait()
            weight = w[b - NEAR_BLOCKS]
        owner = owner_s[b]
        rank = seen[owner]
        seen[owner] = rank + 1
        nodes = in_ref[pl.ds(owner * BACK_ROWS + rank * 3, 3), :].astype(jnp.bfloat16)
        out_ref[:, b, :] = lax.dot_general(
            nodes, weight, (((1,), (1,)), ((), ())), preferred_element_type=jnp.float32
        )


def wall_step(owners, arrived, first_weights, weights):
    return pl.pallas_call(
        wall_body,
        out_shape=shape((3, NB, CX)),
        in_specs=[ANY, VMEM, VMEM, ANY],
        out_specs=VMEM,
        scratch_shapes=[
            pltpu.SMEM((NB,), jnp.int32),
            pltpu.VMEM((NB - NEAR_BLOCKS, CX, SN), jnp.bfloat16),
            pltpu.SMEM((OWNERS,), jnp.int32),
            pltpu.SemaphoreType.DMA((6,)),
            pltpu.SemaphoreType.DMA,
        ],
        cost_estimate=cost(20_000_000, 2_500_000),
        compiler_params=pltpu.CompilerParams(vmem_limit_bytes=16 * 1024 * 1024),
        name="wall",
    )(far(owners), held(arrived), held(first_weights), far(weights))


def collide_body(
    pop_hbm,
    new_hbm,
    rel_ref,
    xp_ref,
    xm_ref,
    yp_ref,
    ym_ref,
    zp_ref,
    zm_ref,
    edge_ref,
    yz_ref,
    pop,
    packed,
    still,
    turned_to,
    sem,
    pop_sem,
):
    arriving = [
        pltpu.make_async_copy(pop_hbm.at[:, z], pop.at[:, z], pop_sem.at[z]) for z in range(CZ)
    ]
    for copy in arriving:
        copy.start()
    lane = lax.broadcasted_iota(jnp.int32, (8, 128), 1)
    for z in range(CZ):
        arriving[z].wait()
        for t in range(CY // 8):
            rows = pl.ds(t * 8, 8)
            f = [pop[d, z, rows, :] for d in range(19)]
            density = f[0]
            for d in range(1, 19):
                density = density + f[d]
            inverse = 1.0 / density
            v = [signed_sum(f, k) * inverse for k in range(3)]
            speed_square = v[0] * v[0] + v[1] * v[1] + v[2] * v[2]
            base = 1.0 - 1.5 * speed_square
            weighted = {w: (relaxation * w) * density for w in set(lattice_weight)}
            pack = jnp.zeros((8, 128), jnp.float32)
            for d in range(19):
                c = lattice_velocity[d]
                projected = None
                for k in range(3):
                    if c[k] != 0:
                        term = v[k] if c[k] > 0 else -v[k]
                        projected = term if projected is None else projected + term
                bracket = base
                if projected is not None:
                    bracket = bracket + projected * (3.0 + 4.5 * projected)
                value = (1.0 - relaxation) * f[d] + weighted[lattice_weight[d]] * bracket
                if c[0] > 0:
                    i = XP.index(d)
                    value = pltpu.roll(value, 1, 1)
                    edge = value if i == 0 else pltpu.roll(value, i, 1)
                    pack = jnp.where(lane == i, edge, pack)
                elif c[0] < 0:
                    i = 8 + XM.index(d)
                    value = pltpu.roll(value, 127, 1)
                    pack = jnp.where(lane == i, pltpu.roll(value, i + 1, 1), pack)
                if c[0] != 0:
                    rel_ref[MOVING.index(d), z, rows, :] = value
                else:
                    still[STILL.index(d), z, rows, :] = value
            packed[pl.ds(z * CY + t * 8, 8), :] = pack

    for h in range(2):
        turned = packed[h * 128 : h * 128 + 128, :].T
        xp_ref[:, h * 128 : h * 128 + 128] = turned[0:8]
        xm_ref[:, h * 128 : h * 128 + 128] = turned[8:16]

    copies = []
    for i, d in enumerate(STILL):
        _, cy, cz = lattice_velocity[d]
        first, count = (1, CZ - 1) if cz > 0 else (0, CZ - 1) if cz < 0 else (0, CZ)
        if cy == 0:
            source = still.at[i, pl.ds(first - cz, count)]
        else:
            spread(
                d, lambda z: still[i, z], turned_to.at[i], edge_ref.at[TURNED.index(d)],
                yp_ref, ym_ref, zp_ref, zm_ref,
            )
            source = turned_to.at[i, pl.ds(first, count)]
        if d in DIAGONAL:
            at = CZ - 1 if cz > 0 else 0
            line = CY - 1 if cy > 0 else 0
            j = DIAGONAL.index(d)
            yz_ref[j : j + 1, :] = still[i, at, line : line + 1, :]
        copy = pltpu.make_async_copy(source, new_hbm.at[d, pl.ds(first, count)], sem.at[i])
        copy.start()
        copies.append(copy)
    zp_ref[ZP.index(5)] = still[STILL.index(5), CZ - 1]
    zm_ref[ZM.index(6)] = still[STILL.index(6), 0]
    for copy in copies:
        copy.wait()


def spread(d, plane_of, res, edge, yp_ref, ym_ref, zp_ref, zm_ref):
    _, cy, cz = lattice_velocity[d]
    for z in range(CZ):
        value = plane_of(z)
        if cy > 0:
            yp_ref[z, YP.index(d) : YP.index(d) + 1, :] = value[CY - 1 : CY]
            value = pltpu.roll(value, 1, 0)
        elif cy < 0:
            ym_ref[z, YM.index(d) : YM.index(d) + 1, :] = value[0:1]
            value = pltpu.roll(value, CY - 1, 0)
        if 0 <= z + cz < CZ:
            res[z + cz] = value
            if cy > 0:
                edge[z + cz] = value[:8]
            elif cy < 0:
                edge[z + cz] = value[CY - 8 :]
        elif cz > 0:
            zp_ref[ZP.index(d)] = value
        else:
            zm_ref[ZM.index(d)] = value


def collide_step(populations):
    return pl.pallas_call(
        collide_body,
        out_shape=(
            shape((19, CZ, CY, CX)),
            near((10, CZ, CY, CX)),
            near((8, ROWS)),
            near((8, ROWS)),
            near((CZ, 8, CX)),
            near((CZ, 8, CX)),
            near((5, CY, CX)),
            near((5, CY, CX)),
            near((6, CZ, 8, CX)),
            near((8, CX)),
        ),
        in_specs=[ANY],
        out_specs=(ANY,) + (VMEM,) * 9,
        scratch_shapes=[
            pltpu.VMEM((19, CZ, CY, CX), jnp.float32),
            pltpu.VMEM((ROWS, 128), jnp.float32),
            pltpu.VMEM((9, CZ, CY, CX), jnp.float32),
            pltpu.VMEM((9, CZ, CY, CX), jnp.float32),
            pltpu.SemaphoreType.DMA((9,)),
            pltpu.SemaphoreType.DMA((CZ,)),
        ],
        cost_estimate=cost(10_000_000, 5_000_000),
        compiler_params=pltpu.CompilerParams(vmem_limit_bytes=16 * 1024 * 1024),
        name="collide",
    )(far(populations))


def stream_body(
    new_in,
    w_hbm,
    rel,
    lo_ref,
    hi_ref,
    yp_in,
    ym_in,
    zp_in,
    zm_in,
    new_hbm,
    yp_ref,
    ym_ref,
    zp_ref,
    zm_ref,
    edge_ref,
    w_ref,
    res,
    cols,
    sem,
    w_sem,
):
    w_copy = pltpu.make_async_copy(w_hbm.at[pl.ds(0, NEAR_BLOCKS)], w_ref, w_sem)
    w_copy.start()
    yp_ref[...] = yp_in[...]
    ym_ref[...] = ym_in[...]
    zp_ref[...] = zp_in[...]
    zm_ref[...] = zm_in[...]
    pad = jnp.zeros((120, 128), jnp.float32)
    for h in range(2):
        for side, ref in enumerate((lo_ref, hi_ref)):
            block = jnp.concatenate([ref[:, h * 128 : h * 128 + 128], pad], axis=0)
            cols[side, h * 128 : h * 128 + 128, :] = block.T
    lane = lax.broadcasted_iota(jnp.int32, (CY, CX), 1)
    copies = []
    for j, d in enumerate(MOVING):
        cx, cy, cz = lattice_velocity[d]
        side, i, at = (0, j, 0) if cx > 0 else (1, j - 5, CX - 1)

        def plane(z):
            column = jnp.broadcast_to(cols[side, z * CY : (z + 1) * CY, i : i + 1], (CY, CX))
            return jnp.where(lane == at, column, rel[j, z])

        edge = edge_ref.at[BENT.index(d)] if cy != 0 else None
        spread(d, plane, res.at[j], edge, yp_ref, ym_ref, zp_ref, zm_ref)
        first, count = (1, CZ - 1) if cz > 0 else (0, CZ - 1) if cz < 0 else (0, CZ)
        planes = pl.ds(first, count)
        copy = pltpu.make_async_copy(res.at[j, planes], new_hbm.at[d, planes], sem.at[j])
        copy.start()
        copies.append(copy)
    w_copy.wait()
    for copy in copies:
        copy.wait()


def stream_step(new, weights, moving, below, above, faces):
    return pl.pallas_call(
        stream_body,
        out_shape=(
            shape((19, CZ, CY, CX)),
            near((CZ, 8, CX)),
            near((CZ, 8, CX)),
            near((5, CY, CX)),
            near((5, CY, CX)),
            near((4, CZ, 8, CX)),
            pltpu.VMEM((NEAR_BLOCKS, CX, SN), jnp.bfloat16),
        ),
        in_specs=[ANY] * 2 + [VMEM] * 7,
        out_specs=(ANY,) + (VMEM,) * 6,
        input_output_aliases={0: 0},
        scratch_shapes=[
            pltpu.VMEM((10, CZ, CY, CX), jnp.float32),
            pltpu.VMEM((2, ROWS, 128), jnp.float32),
            pltpu.SemaphoreType.DMA((10,)),
            pltpu.SemaphoreType.DMA,
        ],
        cost_estimate=cost(10_000_000, 5_000_000),
        compiler_params=pltpu.CompilerParams(vmem_limit_bytes=16 * 1024 * 1024),
        name="stream",
    )(new, far(weights), held(moving), held(below), held(above), *[held(f) for f in faces])


def finish_body(
    new_in, still_ref, moving_ref, ylo, yhi, zlo, zhi, back_ref, new_hbm, tiles, planes, sem
):
    b, e = lax.axis_index("gy"), lax.axis_index("gz")
    copies = []

    def send(source, target):
        copy = pltpu.make_async_copy(source, target, sem.at[len(copies)])
        copy.start()
        copies.append(copy)

    for sign, dirs, halo, at in ((1, ZP, zlo, 0), (-1, ZM, zhi, CZ - 1)):
        for j, d in enumerate(dirs):
            if d in DIAGONAL:
                cy = lattice_velocity[d][1]
                chunk = lax.rem(b - cy + 4, 4) * 16 + lax.rem(e - sign + 16, 16)
                slot = DIAGONAL.index(d)
                line = 0 if cy > 0 else CY - 1
                planes[slot] = halo[j]
                planes[slot, line : line + 1, :] = back_ref[pl.ds(chunk * BACK_ROWS + 6, 1), :]
                send(planes.at[slot], new_hbm.at[d, at])
            else:
                send(halo.at[j], new_hbm.at[d, at])
    for j, d in enumerate(YP + YM):
        cx, cy, cz = lattice_velocity[d]
        ref, i, at = (ylo, j, 0) if cy > 0 else (yhi, j - 5, CY - 1)
        edge = still_ref.at[TURNED.index(d)] if cx == 0 else moving_ref.at[BENT.index(d)]
        for z in range(CZ):
            if 0 <= z + cz < CZ:
                tiles[j, z + cz] = edge[z + cz]
                tiles[j, z + cz, at % 8 : at % 8 + 1, :] = ref[z, i : i + 1, :]
        first, count = (1, CZ - 1) if cz > 0 else (0, CZ - 1) if cz < 0 else (0, CZ)
        inside = pl.ds(first, count)
        send(tiles.at[j, inside], new_hbm.at[d, inside, pl.ds(at // 8 * 8, 8)])
    for copy in copies:
        copy.wait()


def finish_step(new, still, moving, ylo, yhi, zlo, zhi, back):
    return pl.pallas_call(
        finish_body,
        out_shape=shape((19, CZ, CY, CX)),
        in_specs=[ANY] + [VMEM] * 7,
        out_specs=ANY,
        input_output_aliases={0: 0},
        scratch_shapes=[
            pltpu.VMEM((10, CZ, 8, CX), jnp.float32),
            pltpu.VMEM((4, CY, CX), jnp.float32),
            pltpu.SemaphoreType.DMA((20,)),
        ],
        cost_estimate=cost(100_000, 1_000_000),
        compiler_params=pltpu.CompilerParams(vmem_limit_bytes=16 * 1024 * 1024),
        name="finish",
    )(new, *[held(x) for x in (still, moving, ylo, yhi, zlo, zhi, back)])


def from_behind(value, axis, steps):
    count = lax.axis_size(axis)
    pairs = [(source, (source + steps) % count) for source in range(count)]
    return lax.ppermute(value, axis, pairs)


def exchange(value):
    return lax.all_to_all(value, ("gy", "gz"), split_axis=0, concat_axis=0, tiled=True)


def body(
    populations, rbf_weights, owner_map, shell_slot, compliance, neighbour_compliance, interface_row
):
    owners = owner_map.reshape(NB)
    slots = shell_slot.reshape(NB)
    outgoing = send_forces(
        interface_row, owners, slots, populations.reshape(19, ROWS, CX), rbf_weights
    )
    incoming = exchange(outgoing.reshape(OWNERS, 1, OUT_ROWS * 128))
    new, relaxed, xp, xm, yp, ym, zp, zm, still, lines = collide_step(populations)
    xlo = from_behind(xp, "gx", 1)
    xhi = from_behind(xm, "gx", -1)
    displacement, back = owner_step(
        incoming.reshape(OWNERS * OUT_ROWS, 128), compliance, neighbour_compliance, lines
    )
    arrived = exchange(back.reshape(OWNERS, 1, BACK_ROWS * 128))
    new, yp, ym, zp, zm, bent, weights = stream_step(
        new, rbf_weights, relaxed, xlo, xhi, (yp, ym, zp, zm)
    )
    ylo = from_behind(yp, "gy", 1)
    yhi = from_behind(ym, "gy", -1)
    zlo = from_behind(zp, "gz", 1)
    zhi = from_behind(zm, "gz", -1)
    arrived = arrived.reshape(OWNERS * BACK_ROWS, 128)
    wall_motion = wall_step(owners, arrived, weights, rbf_weights)
    new = finish_step(new, still, bent, ylo, yhi, zlo, zhi, arrived)
    return (new, displacement.transpose(1, 0, 2), wall_motion.transpose(1, 0, 2))


def solution(mesh):
    return jax.shard_map(
        body,
        mesh=mesh,
        in_specs=(
            P(None, "gz", "gy", "gx"),
            P(("gx", "gy", "gz"), None, None),
            P(("gx", "gy", "gz"), None),
            P(("gx", "gy", "gz"), None),
            P(("gx", "gy", "gz"), None, None),
            P(("gx", "gy", "gz"), None),
            P(("gx", "gy", "gz")),
        ),
        out_specs=(
            P(None, "gz", "gy", "gx"),
            P(("gx", "gy", "gz"), None, None),
            P(("gx", "gy", "gz"), None, None),
        ),
        check_vma=False,
    )
```

```python
import jax
import jax.numpy as jnp
from jax import lax
from jax.experimental import pallas as pl
from jax.experimental.pallas import tpu as pltpu
from jax.sharding import PartitionSpec as P


lattice_velocity = (
    (0, 0, 0),
    (1, 0, 0),
    (-1, 0, 0),
    (0, 1, 0),
    (0, -1, 0),
    (0, 0, 1),
    (0, 0, -1),
    (1, 1, 0),
    (-1, -1, 0),
    (1, -1, 0),
    (-1, 1, 0),
    (1, 0, 1),
    (-1, 0, -1),
    (1, 0, -1),
    (-1, 0, 1),
    (0, 1, 1),
    (0, -1, -1),
    (0, 1, -1),
    (0, -1, 1),
)
lattice_weight = (1.0 / 3.0,) + (1.0 / 18.0,) * 6 + (1.0 / 36.0,) * 12
load_scale = 30.0
relaxation = 1.6

CZ, CY, CX = 8, 32, 128
ROWS = CZ * CY
NB, SB, SN = 64, 8, 128
OWNERS = 64
NEAR_BLOCKS = 32
HEAD = 2
OUT_ROWS = 10
BACK_ROWS = 7

VMEM = pl.BlockSpec(memory_space=pltpu.VMEM)
SMEM = pl.BlockSpec(memory_space=pltpu.SMEM)
ANY = pl.BlockSpec(memory_space=pl.ANY)


def moved(component, sign):
    return [d for d in range(19) if lattice_velocity[d][component] == sign]


XP, XM = moved(0, 1), moved(0, -1)
YP, YM = moved(1, 1), moved(1, -1)
ZP, ZM = moved(2, 1), moved(2, -1)
MOVING = XP + XM
PAIRS = list(range(1, 19, 2))
STILL = moved(0, 0)
TURNED = [d for d in STILL if lattice_velocity[d][1] != 0]
BENT = [d for d in MOVING if lattice_velocity[d][1] != 0]
DIAGONAL = [d for d in TURNED if lattice_velocity[d][2] != 0]


def signed_sum(values, component):
    total = None
    for d in values:
        c = lattice_velocity[d][component]
        if c == 0:
            continue
        if total is None:
            total = values[d]
        elif c > 0:
            total = total + values[d]
        else:
            total = total - values[d]
    return total


def signed_total(v, c):
    total = None
    for k in range(3):
        if c[k] != 0:
            term = v[k] if c[k] > 0 else -v[k]
            total = term if total is None else total + term
    return total


def shape(dims, dtype=jnp.float32):
    return jax.ShapeDtypeStruct(dims, dtype)


def near(dims):
    return pltpu.VMEM(dims, jnp.float32)


def held(value):
    return pltpu.with_memory_space_constraint(value, pltpu.VMEM)


def far(value):
    return pltpu.with_memory_space_constraint(value, pltpu.HBM)


def cost(flops, moved_bytes):
    return pl.CostEstimate(flops=flops, bytes_accessed=moved_bytes, transcendentals=0)


def forces_body(
    row_hbm,
    owner_hbm,
    slot_hbm,
    pop_hbm,
    w_hbm,
    out_ref,
    head,
    place_ref,
    row_s,
    owner_v,
    slot_v,
    pop,
    w,
    mom,
    made,
    pop_sem,
    w_sem,
    in_sem,
):
    parts = 4
    integers = [
        pltpu.make_async_copy(a, b, in_sem.at[i])
        for i, (a, b) in enumerate(((owner_hbm, owner_v), (slot_hbm, slot_v), (row_hbm, row_s)))
    ]
    pop_copies = []
    for c in range(parts):
        rows = pl.ds(c * (ROWS // parts), ROWS // parts)
        target = head if c == 0 else pop.at[:, pl.ds((c - 1) * (ROWS // parts), ROWS // parts)]
        pop_copies.append(pltpu.make_async_copy(pop_hbm.at[:, rows], target, pop_sem.at[c]))
    w_copies = []
    for c in range(parts):
        blocks = pl.ds(c * (NB // parts), NB // parts)
        w_copies.append(pltpu.make_async_copy(w_hbm.at[blocks], w.at[blocks], w_sem.at[c]))
    for copy in integers + pop_copies + w_copies:
        copy.start()
    for copy in integers:
        copy.wait()

    def iota(dims, axis):
        return lax.broadcasted_iota(jnp.int32, dims, axis).astype(jnp.float32)

    def number(flags):
        return jnp.where(flags, 1.0, 0.0)

    square = (NB, NB)
    owner = owner_v[...].astype(jnp.float32)
    slot = slot_v[...].astype(jnp.float32)
    across = jnp.broadcast_to(owner, square)
    diagonal = iota(square, 0) == iota(square, 1)
    owner_down = jnp.sum(jnp.where(diagonal, across, 0.0), axis=1, keepdims=True)
    same = jnp.broadcast_to(owner_down, square) == across
    rank = jnp.sum(number(same & (iota(square, 0) < iota(square, 1))), axis=0, keepdims=True)
    rank_down = jnp.sum(
        number(same & (iota(square, 1) < iota(square, 0))), axis=1, keepdims=True
    )
    target = jnp.broadcast_to(owner + OWNERS * rank, (2 * OWNERS, NB))
    place = number(target == iota((2 * OWNERS, NB), 0))
    target_down = jnp.broadcast_to(owner_down + OWNERS * rank_down, (NB, 2 * OWNERS))
    place_ref[...] = number(target_down == iota((NB, 2 * OWNERS), 1))
    last = jnp.broadcast_to(slot, square) == SB - 1
    shared = number((across + 1.0 == iota(square, 0)) & last)
    left = jnp.concatenate([place, shared], axis=0).astype(jnp.bfloat16)
    tags = jnp.sum(place * (jnp.broadcast_to(slot, (2 * OWNERS, NB)) + 1.0), axis=1, keepdims=True)
    lane = lax.broadcasted_iota(jnp.int32, (OWNERS, 128), 1)
    first = jnp.broadcast_to(tags[:OWNERS], (OWNERS, 128))
    second = jnp.broadcast_to(tags[OWNERS:], (OWNERS, 128))
    out_ref[pl.ds(9, OWNERS, stride=OUT_ROWS), :] = jnp.where(
        lane == 0, first, jnp.where(lane == 1, second, 0.0)
    )

    for c in range(parts):
        pop_copies[c].wait()
        for t in range(c * (ROWS // parts // 8), (c + 1) * (ROWS // parts // 8)):
            ref, at = (head, t * 8) if c == 0 else (pop, t * 8 - ROWS // parts)
            values = [ref[d, at : at + 8, :] for d in range(19)]
            gaps = {d: values[d] - values[d + 1] for d in PAIRS}
            for k in range(3):
                mom[pl.ds(t * 64 + k, 8, stride=8), :] = load_scale * signed_sum(gaps, k)
    for b in range(NB):
        if b % (NB // parts) == 0:
            w_copies[b // (NB // parts)].wait()
        traction = mom[pl.ds(pl.multiple_of(row_s[b] * 8, 8), 8), :].astype(jnp.bfloat16)
        made[b * 8 : b * 8 + 8, :] = jnp.dot(traction, w[b], preferred_element_type=jnp.float32)
    for k in range(3):
        high, low = two_parts(made[pl.ds(k, NB, stride=8), :])
        rows = jnp.dot(left, high, preferred_element_type=jnp.float32)
        rows = rows + jnp.dot(left, low, preferred_element_type=jnp.float32)
        for g in range(3):
            out_ref[pl.ds(3 * g + k, OWNERS, stride=OUT_ROWS), :] = rows[
                g * OWNERS : (g + 1) * OWNERS
            ]


def send_forces(rows, owners, slots, populations, weights):
    return pl.pallas_call(
        forces_body,
        out_shape=(
            near((OWNERS * OUT_ROWS, 128)),
            near((19, HEAD * CY, CX)),
            near((NB, 2 * OWNERS)),
        ),
        in_specs=[ANY] * 5,
        out_specs=(VMEM, VMEM, VMEM),
        scratch_shapes=[
            pltpu.SMEM((NB,), jnp.int32),
            pltpu.VMEM((1, NB), jnp.int32),
            pltpu.VMEM((1, NB), jnp.int32),
            pltpu.VMEM((19, ROWS - HEAD * CY, CX), jnp.float32),
            pltpu.VMEM((NB, CX, SN), jnp.bfloat16),
            pltpu.VMEM((ROWS * 8, CX), jnp.float32),
            pltpu.VMEM((NB * 8, SN), jnp.float32),
            pltpu.SemaphoreType.DMA((4,)),
            pltpu.SemaphoreType.DMA((4,)),
            pltpu.SemaphoreType.DMA((3,)),
        ],
        cost_estimate=cost(50_000_000, 5_000_000),
        compiler_params=pltpu.CompilerParams(vmem_limit_bytes=16 * 1024 * 1024),
        name="forces",
    )(far(rows), far(owners), far(slots), far(populations), far(weights))


def two_parts(x):
    high = x.astype(jnp.bfloat16)
    return high, (x - high.astype(jnp.float32)).astype(jnp.bfloat16)


def owner_body(in_ref, comp_ref, near_ref, yz_ref, disp_ref, back_ref, left, right):

    b, e = lax.axis_index("gy"), lax.axis_index("gz")
    for j, d in enumerate(DIAGONAL):
        _, cy, cz = lattice_velocity[d]
        chunk = lax.rem(b + cy + 4, 4) * 16 + lax.rem(e + cz + 16, 16)
        back_ref[pl.ds(chunk * BACK_ROWS + 6, 1), :] = yz_ref[j : j + 1, :]

    def rows_of(j):
        return in_ref[pl.ds(j, OWNERS, stride=OUT_ROWS), :]

    def mm(a, b):
        return jnp.dot(a, b, preferred_element_type=jnp.float32)

    tags = rows_of(9)
    lane = lax.broadcasted_iota(jnp.int32, (OWNERS, 128), 1).astype(jnp.float32) + 1.0
    chosen = jnp.concatenate(
        [
            (jnp.broadcast_to(tags[:, r : r + 1], (OWNERS, 128)) == lane).astype(jnp.float32)
            for r in range(2)
        ],
        axis=0,
    )
    select = chosen.T[:SB].astype(jnp.bfloat16)
    left[...] = jnp.zeros(left.shape, jnp.float32)
    for k in range(3):
        arrived = jnp.concatenate([rows_of(k), rows_of(3 + k)], axis=0)
        high, low = two_parts(arrived)
        loads = mm(select, high) + mm(select, low)
        high, low = two_parts(loads)
        left[pl.ds(k, SB, stride=8), :] = high.astype(jnp.float32)
        left[pl.ds(3 + k, SB, stride=8), :] = low.astype(jnp.float32)
        shared = jnp.sum(rows_of(6 + k), axis=0, keepdims=True)
        high, low = two_parts(shared)
        left[SB * 8 + k : SB * 8 + k + 1, :] = high.astype(jnp.float32)
        left[SB * 8 + 3 + k : SB * 8 + 4 + k, :] = low.astype(jnp.float32)

    def product(s, matrix):
        high, low = two_parts(matrix)
        rows = left[s * 8 : s * 8 + 8, :].astype(jnp.bfloat16)
        first = mm(rows, high)
        return first[:3] + first[3:6] + mm(rows, low)[:3]

    for s in range(SB):
        moved_by = product(s, comp_ref[s])
        if s == 0:
            moved_by = moved_by + product(SB, near_ref[...])
        disp_ref[:, s, :] = moved_by
        right[s * 8 : s * 8 + 3, :] = moved_by
    chosen = chosen.astype(jnp.bfloat16)
    for k in range(3):
        nodes = right[pl.ds(k, SB, stride=8), :].astype(jnp.bfloat16).astype(jnp.float32)
        nodes = jnp.concatenate([nodes, jnp.zeros((128 - SB, 128), jnp.float32)], axis=0)
        back = mm(chosen, nodes.astype(jnp.bfloat16))
        for r in range(2):
            back_ref[pl.ds(3 * r + k, OWNERS, stride=BACK_ROWS), :] = back[
                r * OWNERS : (r + 1) * OWNERS
            ]


def owner_step(arrived, compliance, neighbour, lines):
    return pl.pallas_call(
        owner_body,
        out_shape=(shape((3, SB, SN)), near((OWNERS * BACK_ROWS, 128))),
        in_specs=[VMEM] * 4,
        out_specs=(VMEM, VMEM),
        scratch_shapes=[
            pltpu.VMEM((SB * 8 + 8, 128), jnp.float32),
            pltpu.VMEM((SB * 8, 128), jnp.float32),
        ],
        cost_estimate=cost(20_000_000, 1_200_000),
        compiler_params=pltpu.CompilerParams(vmem_limit_bytes=16 * 1024 * 1024),
        name="owner",
    )(held(arrived), held(compliance), held(neighbour), held(lines))


def wall_body(place_ref, in_ref, w_near, w_hbm, out_ref, w, nodes, w_sem):
    parts = 4
    size = (NB - NEAR_BLOCKS) // parts
    w_copies = []
    for c in range(parts):
        w_copies.append(
            pltpu.make_async_copy(
                w_hbm.at[pl.ds(NEAR_BLOCKS + c * size, size)], w.at[pl.ds(c * size, size)], w_sem.at[c]
            )
        )
    for copy in w_copies:
        copy.start()
    place = place_ref[...].astype(jnp.bfloat16)
    for k in range(3):
        arrived = jnp.concatenate(
            [in_ref[pl.ds(3 * r + k, OWNERS, stride=BACK_ROWS), :] for r in range(2)], axis=0
        )
        nodes[pl.ds(k, NB, stride=8), :] = jnp.dot(
            place, arrived.astype(jnp.bfloat16), preferred_element_type=jnp.float32
        )
    for b in range(NB):
        if b < NEAR_BLOCKS:
            weight = w_near[b]
        else:
            if (b - NEAR_BLOCKS) % size == 0:
                w_copies[(b - NEAR_BLOCKS) // size].wait()
            weight = w[b - NEAR_BLOCKS]
        motion = lax.dot_general(
            nodes[b * 8 : b * 8 + 8, :].astype(jnp.bfloat16),
            weight,
            (((1,), (1,)), ((), ())),
            preferred_element_type=jnp.float32,
        )
        out_ref[:, b, :] = motion[:3]


def wall_step(place, arrived, first_weights, weights):
    return pl.pallas_call(
        wall_body,
        out_shape=shape((3, NB, CX)),
        in_specs=[VMEM, VMEM, VMEM, ANY],
        out_specs=VMEM,
        scratch_shapes=[
            pltpu.VMEM((NB - NEAR_BLOCKS, CX, SN), jnp.bfloat16),
            pltpu.VMEM((NB * 8, SN), jnp.float32),
            pltpu.SemaphoreType.DMA((4,)),
        ],
        cost_estimate=cost(20_000_000, 2_500_000),
        compiler_params=pltpu.CompilerParams(vmem_limit_bytes=16 * 1024 * 1024),
        name="wall",
    )(held(place), held(arrived), held(first_weights), far(weights))


def collide_body(
    pop_hbm,
    head,
    new_hbm,
    rel_ref,
    xp_ref,
    xm_ref,
    yp_ref,
    ym_ref,
    zp_ref,
    zm_ref,
    edge_ref,
    yz_ref,
    pop,
    packed,
    still,
    turned_to,
    sem,
    pop_sem,
):
    arriving = [
        pltpu.make_async_copy(pop_hbm.at[:, z], pop.at[:, z - HEAD], pop_sem.at[z])
        for z in range(HEAD, CZ)
    ]
    for copy in arriving:
        copy.start()
    lane = lax.broadcasted_iota(jnp.int32, (8, 128), 1)
    for z in range(CZ):
        if z >= HEAD:
            arriving[z - HEAD].wait()
        for t in range(CY // 8):
            rows = pl.ds(t * 8, 8)
            if z < HEAD:
                f = [head[d, z * CY + t * 8 : z * CY + t * 8 + 8, :] for d in range(19)]
            else:
                f = [pop[d, z - HEAD, rows, :] for d in range(19)]
            sums = {d: f[d] + f[d + 1] for d in PAIRS}
            gaps = {d: f[d] - f[d + 1] for d in PAIRS}
            density = f[0]
            for d in PAIRS:
                density = density + sums[d]
            inverse = 1.0 / density
            v = [signed_sum(gaps, k) * inverse for k in range(3)]
            speed_square = v[0] * v[0] + v[1] * v[1] + v[2] * v[2]
            base = 1.0 - 1.5 * speed_square
            share = {w: (relaxation * w) * density for w in set(lattice_weight)}
            steady = {w: share[w] * base for w in set(lattice_weight)}
            slope = {w: (3.0 * relaxation * w) * density for w in set(lattice_weight)}
            values = {0: (1.0 - relaxation) * f[0] + steady[lattice_weight[0]]}
            for d in PAIRS:
                w = lattice_weight[d]
                projected = signed_total(v, lattice_velocity[d])
                odd = slope[w] * projected
                even = steady[w] + 1.5 * (odd * projected)
                values[d] = (1.0 - relaxation) * f[d] + (even + odd)
                values[d + 1] = (1.0 - relaxation) * f[d + 1] + (even - odd)
            pack = jnp.zeros((8, 128), jnp.float32)
            for d in range(19):
                c = lattice_velocity[d]
                value = values[d]
                if c[0] > 0:
                    i = XP.index(d)
                    value = pltpu.roll(value, 1, 1)
                    edge = value if i == 0 else pltpu.roll(value, i, 1)
                    pack = jnp.where(lane == i, edge, pack)
                elif c[0] < 0:
                    i = 8 + XM.index(d)
                    value = pltpu.roll(value, 127, 1)
                    pack = jnp.where(lane == i, pltpu.roll(value, i + 1, 1), pack)
                if c[0] != 0:
                    rel_ref[MOVING.index(d), z, rows, :] = value
                else:
                    still[STILL.index(d), z, rows, :] = value
            packed[pl.ds(z * CY + t * 8, 8), :] = pack

    for h in range(2):
        turned = packed[h * 128 : h * 128 + 128, :].T
        xp_ref[:, h * 128 : h * 128 + 128] = turned[0:8]
        xm_ref[:, h * 128 : h * 128 + 128] = turned[8:16]

    copies = []
    for i, d in enumerate(STILL):
        _, cy, cz = lattice_velocity[d]
        first, count = (1, CZ - 1) if cz > 0 else (0, CZ - 1) if cz < 0 else (0, CZ)
        if cy == 0:
            source = still.at[i, pl.ds(first - cz, count)]
        else:
            spread(
                d, lambda z: still[i, z], turned_to.at[i], edge_ref.at[TURNED.index(d)],
                yp_ref, ym_ref, zp_ref, zm_ref,
            )
            source = turned_to.at[i, pl.ds(first, count)]
        if d in DIAGONAL:
            at = CZ - 1 if cz > 0 else 0
            line = CY - 1 if cy > 0 else 0
            j = DIAGONAL.index(d)
            yz_ref[j : j + 1, :] = still[i, at, line : line + 1, :]
        copy = pltpu.make_async_copy(source, new_hbm.at[d, pl.ds(first, count)], sem.at[i])
        copy.start()
        copies.append(copy)
    zp_ref[ZP.index(5)] = still[STILL.index(5), CZ - 1]
    zm_ref[ZM.index(6)] = still[STILL.index(6), 0]
    for copy in copies:
        copy.wait()


def spread(d, plane_of, res, edge, yp_ref, ym_ref, zp_ref, zm_ref):
    _, cy, cz = lattice_velocity[d]
    for z in range(CZ):
        value = plane_of(z)
        if cy > 0:
            yp_ref[z, YP.index(d) : YP.index(d) + 1, :] = value[CY - 1 : CY]
            value = pltpu.roll(value, 1, 0)
        elif cy < 0:
            ym_ref[z, YM.index(d) : YM.index(d) + 1, :] = value[0:1]
            value = pltpu.roll(value, CY - 1, 0)
        if 0 <= z + cz < CZ:
            res[z + cz] = value
            if cy > 0:
                edge[z + cz] = value[:8]
            elif cy < 0:
                edge[z + cz] = value[CY - 8 :]
        elif cz > 0:
            zp_ref[ZP.index(d)] = value
        else:
            zm_ref[ZM.index(d)] = value


def collide_step(populations, head):
    return pl.pallas_call(
        collide_body,
        out_shape=(
            shape((19, CZ, CY, CX)),
            near((10, CZ, CY, CX)),
            near((8, ROWS)),
            near((8, ROWS)),
            near((CZ, 8, CX)),
            near((CZ, 8, CX)),
            near((5, CY, CX)),
            near((5, CY, CX)),
            near((6, CZ, 8, CX)),
            near((8, CX)),
        ),
        in_specs=[ANY, VMEM],
        out_specs=(ANY,) + (VMEM,) * 9,
        scratch_shapes=[
            pltpu.VMEM((19, CZ - HEAD, CY, CX), jnp.float32),
            pltpu.VMEM((ROWS, 128), jnp.float32),
            pltpu.VMEM((9, CZ, CY, CX), jnp.float32),
            pltpu.VMEM((9, CZ, CY, CX), jnp.float32),
            pltpu.SemaphoreType.DMA((9,)),
            pltpu.SemaphoreType.DMA((CZ,)),
        ],
        cost_estimate=cost(10_000_000, 5_000_000),
        compiler_params=pltpu.CompilerParams(vmem_limit_bytes=16 * 1024 * 1024),
        name="collide",
    )(far(populations), held(head))


def stream_body(
    new_in,
    w_hbm,
    rel,
    lo_ref,
    hi_ref,
    yp_in,
    ym_in,
    zp_in,
    zm_in,
    new_hbm,
    yp_ref,
    ym_ref,
    zp_ref,
    zm_ref,
    edge_ref,
    w_ref,
    res,
    cols,
    sem,
    w_sem,
):
    w_copy = pltpu.make_async_copy(w_hbm.at[pl.ds(0, NEAR_BLOCKS)], w_ref, w_sem)
    w_copy.start()
    yp_ref[...] = yp_in[...]
    ym_ref[...] = ym_in[...]
    zp_ref[...] = zp_in[...]
    zm_ref[...] = zm_in[...]
    pad = jnp.zeros((120, 128), jnp.float32)
    for h in range(2):
        for side, ref in enumerate((lo_ref, hi_ref)):
            block = jnp.concatenate([ref[:, h * 128 : h * 128 + 128], pad], axis=0)
            cols[side, h * 128 : h * 128 + 128, :] = block.T
    lane = lax.broadcasted_iota(jnp.int32, (CY, CX), 1)
    copies = []
    for j, d in enumerate(MOVING):
        cx, cy, cz = lattice_velocity[d]
        side, i, at = (0, j, 0) if cx > 0 else (1, j - 5, CX - 1)

        def plane(z):
            column = jnp.broadcast_to(cols[side, z * CY : (z + 1) * CY, i : i + 1], (CY, CX))
            return jnp.where(lane == at, column, rel[j, z])

        edge = edge_ref.at[BENT.index(d)] if cy != 0 else None
        spread(d, plane, res.at[j], edge, yp_ref, ym_ref, zp_ref, zm_ref)
        first, count = (1, CZ - 1) if cz > 0 else (0, CZ - 1) if cz < 0 else (0, CZ)
        planes = pl.ds(first, count)
        copy = pltpu.make_async_copy(res.at[j, planes], new_hbm.at[d, planes], sem.at[j])
        copy.start()
        copies.append(copy)
    w_copy.wait()
    for copy in copies:
        copy.wait()


def stream_step(new, weights, moving, below, above, faces):
    return pl.pallas_call(
        stream_body,
        out_shape=(
            shape((19, CZ, CY, CX)),
            near((CZ, 8, CX)),
            near((CZ, 8, CX)),
            near((5, CY, CX)),
            near((5, CY, CX)),
            near((4, CZ, 8, CX)),
            pltpu.VMEM((NEAR_BLOCKS, CX, SN), jnp.bfloat16),
        ),
        in_specs=[ANY] * 2 + [VMEM] * 7,
        out_specs=(ANY,) + (VMEM,) * 6,
        input_output_aliases={0: 0},
        scratch_shapes=[
            pltpu.VMEM((10, CZ, CY, CX), jnp.float32),
            pltpu.VMEM((2, ROWS, 128), jnp.float32),
            pltpu.SemaphoreType.DMA((10,)),
            pltpu.SemaphoreType.DMA,
        ],
        cost_estimate=cost(10_000_000, 5_000_000),
        compiler_params=pltpu.CompilerParams(vmem_limit_bytes=16 * 1024 * 1024),
        name="stream",
    )(new, far(weights), held(moving), held(below), held(above), *[held(f) for f in faces])


def finish_body(
    new_in, still_ref, moving_ref, ylo, yhi, zlo, zhi, back_ref, new_hbm, tiles, planes, sem
):
    b, e = lax.axis_index("gy"), lax.axis_index("gz")
    copies = []

    def send(source, target):
        copy = pltpu.make_async_copy(source, target, sem.at[len(copies)])
        copy.start()
        copies.append(copy)

    for sign, dirs, halo, at in ((1, ZP, zlo, 0), (-1, ZM, zhi, CZ - 1)):
        for j, d in enumerate(dirs):
            if d in DIAGONAL:
                cy = lattice_velocity[d][1]
                chunk = lax.rem(b - cy + 4, 4) * 16 + lax.rem(e - sign + 16, 16)
                slot = DIAGONAL.index(d)
                line = 0 if cy > 0 else CY - 1
                planes[slot] = halo[j]
                planes[slot, line : line + 1, :] = back_ref[pl.ds(chunk * BACK_ROWS + 6, 1), :]
                send(planes.at[slot], new_hbm.at[d, at])
            else:
                send(halo.at[j], new_hbm.at[d, at])
    for j, d in enumerate(YP + YM):
        cx, cy, cz = lattice_velocity[d]
        ref, i, at = (ylo, j, 0) if cy > 0 else (yhi, j - 5, CY - 1)
        edge = still_ref.at[TURNED.index(d)] if cx == 0 else moving_ref.at[BENT.index(d)]
        for z in range(CZ):
            if 0 <= z + cz < CZ:
                tiles[j, z + cz] = edge[z + cz]
                tiles[j, z + cz, at % 8 : at % 8 + 1, :] = ref[z, i : i + 1, :]
        first, count = (1, CZ - 1) if cz > 0 else (0, CZ - 1) if cz < 0 else (0, CZ)
        inside = pl.ds(first, count)
        send(tiles.at[j, inside], new_hbm.at[d, inside, pl.ds(at // 8 * 8, 8)])
    for copy in copies:
        copy.wait()


def finish_step(new, still, moving, ylo, yhi, zlo, zhi, back):
    return pl.pallas_call(
        finish_body,
        out_shape=shape((19, CZ, CY, CX)),
        in_specs=[ANY] + [VMEM] * 7,
        out_specs=ANY,
        input_output_aliases={0: 0},
        scratch_shapes=[
            pltpu.VMEM((10, CZ, 8, CX), jnp.float32),
            pltpu.VMEM((4, CY, CX), jnp.float32),
            pltpu.SemaphoreType.DMA((20,)),
        ],
        cost_estimate=cost(100_000, 1_000_000),
        compiler_params=pltpu.CompilerParams(vmem_limit_bytes=16 * 1024 * 1024),
        name="finish",
    )(new, *[held(x) for x in (still, moving, ylo, yhi, zlo, zhi, back)])


def from_behind(value, axis, steps):
    count = lax.axis_size(axis)
    pairs = [(source, (source + steps) % count) for source in range(count)]
    return lax.ppermute(value, axis, pairs)


def exchange(value):
    return lax.all_to_all(value, ("gy", "gz"), split_axis=0, concat_axis=0, tiled=True)


def body(
    populations, rbf_weights, owner_map, shell_slot, compliance, neighbour_compliance, interface_row
):
    owners = owner_map.reshape(1, NB)
    slots = shell_slot.reshape(1, NB)
    outgoing, head, place = send_forces(
        interface_row, owners, slots, populations.reshape(19, ROWS, CX), rbf_weights
    )
    incoming = exchange(outgoing.reshape(OWNERS, 1, OUT_ROWS * 128))
    new, relaxed, xp, xm, yp, ym, zp, zm, still, lines = collide_step(populations, head)
    xlo = from_behind(xp, "gx", 1)
    xhi = from_behind(xm, "gx", -1)
    displacement, back = owner_step(
        incoming.reshape(OWNERS * OUT_ROWS, 128), compliance, neighbour_compliance, lines
    )
    arrived = exchange(back.reshape(OWNERS, 1, BACK_ROWS * 128))
    new, yp, ym, zp, zm, bent, weights = stream_step(
        new, rbf_weights, relaxed, xlo, xhi, (yp, ym, zp, zm)
    )
    ylo = from_behind(yp, "gy", 1)
    yhi = from_behind(ym, "gy", -1)
    zlo = from_behind(zp, "gz", 1)
    zhi = from_behind(zm, "gz", -1)
    arrived = arrived.reshape(OWNERS * BACK_ROWS, 128)
    wall_motion = wall_step(place, arrived, weights, rbf_weights)
    new = finish_step(new, still, bent, ylo, yhi, zlo, zhi, arrived)
    return (new, displacement.transpose(1, 0, 2), wall_motion.transpose(1, 0, 2))


def solution(mesh):
    return jax.shard_map(
        body,
        mesh=mesh,
        in_specs=(
            P(None, "gz", "gy", "gx"),
            P(("gx", "gy", "gz"), None, None),
            P(("gx", "gy", "gz"), None),
            P(("gx", "gy", "gz"), None),
            P(("gx", "gy", "gz"), None, None),
            P(("gx", "gy", "gz"), None),
            P(("gx", "gy", "gz")),
        ),
        out_specs=(
            P(None, "gz", "gy", "gx"),
            P(("gx", "gy", "gz"), None, None),
            P(("gx", "gy", "gz"), None, None),
        ),
        check_vma=False,
    )
```

```python
import jax
import jax.numpy as jnp
from jax import lax
from jax.experimental import pallas as pl
from jax.experimental.pallas import tpu as pltpu
from jax.sharding import PartitionSpec as P


lattice_velocity = (
    (0, 0, 0),
    (1, 0, 0),
    (-1, 0, 0),
    (0, 1, 0),
    (0, -1, 0),
    (0, 0, 1),
    (0, 0, -1),
    (1, 1, 0),
    (-1, -1, 0),
    (1, -1, 0),
    (-1, 1, 0),
    (1, 0, 1),
    (-1, 0, -1),
    (1, 0, -1),
    (-1, 0, 1),
    (0, 1, 1),
    (0, -1, -1),
    (0, 1, -1),
    (0, -1, 1),
)
lattice_weight = (1.0 / 3.0,) + (1.0 / 18.0,) * 6 + (1.0 / 36.0,) * 12
load_scale = 30.0
relaxation = 1.6

CZ, CY, CX = 8, 32, 128
ROWS = CZ * CY
NB, SB, SN = 64, 8, 128
OWNERS = 64
HEAD = 2
OUT_ROWS = 10
BACK_ROWS = 7

VMEM = pl.BlockSpec(memory_space=pltpu.VMEM)
SMEM = pl.BlockSpec(memory_space=pltpu.SMEM)
ANY = pl.BlockSpec(memory_space=pl.ANY)


def moved(component, sign):
    return [d for d in range(19) if lattice_velocity[d][component] == sign]


XP, XM = moved(0, 1), moved(0, -1)
YP, YM = moved(1, 1), moved(1, -1)
ZP, ZM = moved(2, 1), moved(2, -1)
MOVING = XP + XM
PAIRS = list(range(1, 19, 2))
STILL = moved(0, 0)
TURNED = [d for d in STILL if lattice_velocity[d][1] != 0]
BENT = [d for d in MOVING if lattice_velocity[d][1] != 0]
DIAGONAL = [d for d in TURNED if lattice_velocity[d][2] != 0]


def signed_sum(values, component):
    total = None
    for d in values:
        c = lattice_velocity[d][component]
        if c == 0:
            continue
        if total is None:
            total = values[d]
        elif c > 0:
            total = total + values[d]
        else:
            total = total - values[d]
    return total


def signed_total(v, c):
    total = None
    for k in range(3):
        if c[k] != 0:
            term = v[k] if c[k] > 0 else -v[k]
            total = term if total is None else total + term
    return total


def shape(dims, dtype=jnp.float32):
    return jax.ShapeDtypeStruct(dims, dtype)


def near(dims):
    return pltpu.VMEM(dims, jnp.float32)


def held(value):
    return pltpu.with_memory_space_constraint(value, pltpu.VMEM)


def far(value):
    return pltpu.with_memory_space_constraint(value, pltpu.HBM)


def cost(flops, moved_bytes):
    return pl.CostEstimate(flops=flops, bytes_accessed=moved_bytes, transcendentals=0)


def forces_body(
    row_hbm,
    owner_hbm,
    slot_hbm,
    pop_hbm,
    w_hbm,
    out_ref,
    head,
    place_ref,
    row_s,
    owner_v,
    slot_v,
    pop,
    w,
    mom,
    made,
    pop_sem,
    w_sem,
    in_sem,
):
    parts = 4
    integers = [
        pltpu.make_async_copy(a, b, in_sem.at[i])
        for i, (a, b) in enumerate(((owner_hbm, owner_v), (slot_hbm, slot_v), (row_hbm, row_s)))
    ]
    pop_copies = []
    for c in range(parts):
        rows = pl.ds(c * (ROWS // parts), ROWS // parts)
        target = head if c == 0 else pop.at[:, pl.ds((c - 1) * (ROWS // parts), ROWS // parts)]
        pop_copies.append(pltpu.make_async_copy(pop_hbm.at[:, rows], target, pop_sem.at[c]))
    w_copies = []
    pieces = 8
    for c in range(pieces):
        blocks = pl.ds(c * (NB // pieces), NB // pieces)
        w_copies.append(pltpu.make_async_copy(w_hbm.at[blocks], w.at[blocks], w_sem.at[c]))
    for copy in integers + pop_copies + w_copies:
        copy.start()
    for copy in integers:
        copy.wait()

    def iota(dims, axis):
        return lax.broadcasted_iota(jnp.int32, dims, axis).astype(jnp.float32)

    def number(flags):
        return jnp.where(flags, 1.0, 0.0)

    square = (NB, NB)
    owner = owner_v[...].astype(jnp.float32)
    slot = slot_v[...].astype(jnp.float32)
    across = jnp.broadcast_to(owner, square)
    diagonal = iota(square, 0) == iota(square, 1)
    owner_down = jnp.sum(jnp.where(diagonal, across, 0.0), axis=1, keepdims=True)
    same = jnp.broadcast_to(owner_down, square) == across
    rank = jnp.sum(number(same & (iota(square, 0) < iota(square, 1))), axis=0, keepdims=True)
    rank_down = jnp.sum(
        number(same & (iota(square, 1) < iota(square, 0))), axis=1, keepdims=True
    )
    target = jnp.broadcast_to(owner + OWNERS * rank, (2 * OWNERS, NB))
    place = number(target == iota((2 * OWNERS, NB), 0))
    target_down = jnp.broadcast_to(owner_down + OWNERS * rank_down, (NB, 2 * OWNERS))
    place_ref[...] = number(target_down == iota((NB, 2 * OWNERS), 1))
    last = jnp.broadcast_to(slot, square) == SB - 1
    shared = number((across + 1.0 == iota(square, 0)) & last)
    left = jnp.concatenate([place, shared], axis=0).astype(jnp.bfloat16)
    tags = jnp.sum(place * (jnp.broadcast_to(slot, (2 * OWNERS, NB)) + 1.0), axis=1, keepdims=True)
    lane = lax.broadcasted_iota(jnp.int32, (OWNERS, 128), 1)
    first = jnp.broadcast_to(tags[:OWNERS], (OWNERS, 128))
    second = jnp.broadcast_to(tags[OWNERS:], (OWNERS, 128))
    out_ref[pl.ds(9, OWNERS, stride=OUT_ROWS), :] = jnp.where(
        lane == 0, first, jnp.where(lane == 1, second, 0.0)
    )

    for c in range(parts):
        pop_copies[c].wait()
        for t in range(c * (ROWS // parts // 8), (c + 1) * (ROWS // parts // 8)):
            ref, at = (head, t * 8) if c == 0 else (pop, t * 8 - ROWS // parts)
            values = [ref[d, at : at + 8, :] for d in range(19)]
            gaps = {d: values[d] - values[d + 1] for d in PAIRS}
            for k in range(3):
                mom[pl.ds(t * 64 + k, 8, stride=8), :] = load_scale * signed_sum(gaps, k)
    for b in range(NB):
        if b % (NB // pieces) == 0:
            w_copies[b // (NB // pieces)].wait()
        traction = mom[pl.ds(pl.multiple_of(row_s[b] * 8, 8), 8), :].astype(jnp.bfloat16)
        made[b * 8 : b * 8 + 8, :] = jnp.dot(traction, w[b], preferred_element_type=jnp.float32)
    for k in range(3):
        high, low = two_parts(made[pl.ds(k, NB, stride=8), :])
        rows = jnp.dot(left, high, preferred_element_type=jnp.float32)
        rows = rows + jnp.dot(left, low, preferred_element_type=jnp.float32)
        for g in range(3):
            out_ref[pl.ds(3 * g + k, OWNERS, stride=OUT_ROWS), :] = rows[
                g * OWNERS : (g + 1) * OWNERS
            ]


def send_forces(rows, owners, slots, populations, weights):
    return pl.pallas_call(
        forces_body,
        out_shape=(
            near((OWNERS * OUT_ROWS, 128)),
            near((19, HEAD * CY, CX)),
            near((NB, 2 * OWNERS)),
        ),
        in_specs=[ANY] * 5,
        out_specs=(VMEM, VMEM, VMEM),
        scratch_shapes=[
            pltpu.SMEM((NB,), jnp.int32),
            pltpu.VMEM((1, NB), jnp.int32),
            pltpu.VMEM((1, NB), jnp.int32),
            pltpu.VMEM((19, ROWS - HEAD * CY, CX), jnp.float32),
            pltpu.VMEM((NB, CX, SN), jnp.bfloat16),
            pltpu.VMEM((ROWS * 8, CX), jnp.float32),
            pltpu.VMEM((NB * 8, SN), jnp.float32),
            pltpu.SemaphoreType.DMA((4,)),
            pltpu.SemaphoreType.DMA((8,)),
            pltpu.SemaphoreType.DMA((3,)),
        ],
        cost_estimate=cost(50_000_000, 5_000_000),
        compiler_params=pltpu.CompilerParams(vmem_limit_bytes=16 * 1024 * 1024),
        name="forces",
    )(far(rows), far(owners), far(slots), far(populations), far(weights))


def two_parts(x):
    high = x.astype(jnp.bfloat16)
    return high, (x - high.astype(jnp.float32)).astype(jnp.bfloat16)


def owner_body(in_ref, comp_ref, near_ref, yz_ref, disp_ref, back_ref, left, right):

    b, e = lax.axis_index("gy"), lax.axis_index("gz")
    for j, d in enumerate(DIAGONAL):
        _, cy, cz = lattice_velocity[d]
        chunk = lax.rem(b + cy + 4, 4) * 16 + lax.rem(e + cz + 16, 16)
        back_ref[pl.ds(chunk * BACK_ROWS + 6, 1), :] = yz_ref[j : j + 1, :]

    def rows_of(j):
        return in_ref[pl.ds(j, OWNERS, stride=OUT_ROWS), :]

    def mm(a, b):
        return jnp.dot(a, b, preferred_element_type=jnp.float32)

    tags = rows_of(9)
    lane = lax.broadcasted_iota(jnp.int32, (OWNERS, 128), 1).astype(jnp.float32) + 1.0
    chosen = jnp.concatenate(
        [
            (jnp.broadcast_to(tags[:, r : r + 1], (OWNERS, 128)) == lane).astype(jnp.float32)
            for r in range(2)
        ],
        axis=0,
    )
    select = chosen.T[:SB].astype(jnp.bfloat16)
    left[...] = jnp.zeros(left.shape, jnp.float32)
    for k in range(3):
        arrived = jnp.concatenate([rows_of(k), rows_of(3 + k)], axis=0)
        high, low = two_parts(arrived)
        loads = mm(select, high) + mm(select, low)
        high, low = two_parts(loads)
        left[pl.ds(k, SB, stride=8), :] = high.astype(jnp.float32)
        left[pl.ds(3 + k, SB, stride=8), :] = low.astype(jnp.float32)
        shared = jnp.sum(rows_of(6 + k), axis=0, keepdims=True)
        high, low = two_parts(shared)
        left[SB * 8 + k : SB * 8 + k + 1, :] = high.astype(jnp.float32)
        left[SB * 8 + 3 + k : SB * 8 + 4 + k, :] = low.astype(jnp.float32)

    def product(s, matrix):
        high, low = two_parts(matrix)
        rows = left[s * 8 : s * 8 + 8, :].astype(jnp.bfloat16)
        first = mm(rows, high)
        return first[:3] + first[3:6] + mm(rows, low)[:3]

    for s in range(SB):
        moved_by = product(s, comp_ref[s])
        if s == 0:
            moved_by = moved_by + product(SB, near_ref[...])
        disp_ref[:, s, :] = moved_by
        right[s * 8 : s * 8 + 3, :] = moved_by
    chosen = chosen.astype(jnp.bfloat16)
    for k in range(3):
        nodes = right[pl.ds(k, SB, stride=8), :].astype(jnp.bfloat16).astype(jnp.float32)
        nodes = jnp.concatenate([nodes, jnp.zeros((128 - SB, 128), jnp.float32)], axis=0)
        back = mm(chosen, nodes.astype(jnp.bfloat16))
        for r in range(2):
            back_ref[pl.ds(3 * r + k, OWNERS, stride=BACK_ROWS), :] = back[
                r * OWNERS : (r + 1) * OWNERS
            ]


def owner_step(arrived, compliance, neighbour, lines):
    return pl.pallas_call(
        owner_body,
        out_shape=(shape((3, SB, SN)), near((OWNERS * BACK_ROWS, 128))),
        in_specs=[VMEM] * 4,
        out_specs=(VMEM, VMEM),
        scratch_shapes=[
            pltpu.VMEM((SB * 8 + 8, 128), jnp.float32),
            pltpu.VMEM((SB * 8, 128), jnp.float32),
        ],
        cost_estimate=cost(20_000_000, 1_200_000),
        compiler_params=pltpu.CompilerParams(vmem_limit_bytes=16 * 1024 * 1024),
        name="owner",
    )(held(arrived), held(compliance), held(neighbour), held(lines))


def collide_body(
    pop_hbm,
    head,
    new_hbm,
    rel_ref,
    xp_ref,
    xm_ref,
    yp_ref,
    ym_ref,
    zp_ref,
    zm_ref,
    edge_ref,
    yz_ref,
    pop,
    packed,
    still,
    turned_to,
    sem,
    pop_sem,
):
    arriving = [
        pltpu.make_async_copy(pop_hbm.at[:, z], pop.at[:, z - HEAD], pop_sem.at[z])
        for z in range(HEAD, CZ)
    ]
    for copy in arriving:
        copy.start()
    lane = lax.broadcasted_iota(jnp.int32, (8, 128), 1)
    for z in range(CZ):
        if z >= HEAD:
            arriving[z - HEAD].wait()
        for t in range(CY // 8):
            rows = pl.ds(t * 8, 8)
            if z < HEAD:
                f = [head[d, z * CY + t * 8 : z * CY + t * 8 + 8, :] for d in range(19)]
            else:
                f = [pop[d, z - HEAD, rows, :] for d in range(19)]
            sums = {d: f[d] + f[d + 1] for d in PAIRS}
            gaps = {d: f[d] - f[d + 1] for d in PAIRS}
            density = f[0]
            for d in PAIRS:
                density = density + sums[d]
            inverse = 1.0 / density
            v = [signed_sum(gaps, k) * inverse for k in range(3)]
            speed_square = v[0] * v[0] + v[1] * v[1] + v[2] * v[2]
            base = 1.0 - 1.5 * speed_square
            share = {w: (relaxation * w) * density for w in set(lattice_weight)}
            steady = {w: share[w] * base for w in set(lattice_weight)}
            slope = {w: (3.0 * relaxation * w) * density for w in set(lattice_weight)}
            values = {0: (1.0 - relaxation) * f[0] + steady[lattice_weight[0]]}
            for d in PAIRS:
                w = lattice_weight[d]
                projected = signed_total(v, lattice_velocity[d])
                odd = slope[w] * projected
                even = steady[w] + 1.5 * (odd * projected)
                values[d] = (1.0 - relaxation) * f[d] + (even + odd)
                values[d + 1] = (1.0 - relaxation) * f[d + 1] + (even - odd)
            pack = jnp.zeros((8, 128), jnp.float32)
            for d in range(19):
                c = lattice_velocity[d]
                value = values[d]
                if c[0] > 0:
                    i = XP.index(d)
                    value = pltpu.roll(value, 1, 1)
                    edge = value if i == 0 else pltpu.roll(value, i, 1)
                    pack = jnp.where(lane == i, edge, pack)
                elif c[0] < 0:
                    i = 8 + XM.index(d)
                    value = pltpu.roll(value, 127, 1)
                    pack = jnp.where(lane == i, pltpu.roll(value, i + 1, 1), pack)
                if c[0] != 0:
                    rel_ref[MOVING.index(d), z, rows, :] = value
                else:
                    still[STILL.index(d), z, rows, :] = value
            packed[pl.ds(z * CY + t * 8, 8), :] = pack

    for h in range(2):
        turned = packed[h * 128 : h * 128 + 128, :].T
        xp_ref[:, h * 128 : h * 128 + 128] = turned[0:8]
        xm_ref[:, h * 128 : h * 128 + 128] = turned[8:16]

    copies = []
    for i, d in enumerate(STILL):
        _, cy, cz = lattice_velocity[d]
        first, count = (1, CZ - 1) if cz > 0 else (0, CZ - 1) if cz < 0 else (0, CZ)
        if cy == 0:
            source = still.at[i, pl.ds(first - cz, count)]
        else:
            faces = (yp_ref, ym_ref, zp_ref, zm_ref)
            spread(d, lambda z: still[i, z], turned_to.at[i], edge_ref.at[TURNED.index(d)], faces)
            source = turned_to.at[i, pl.ds(first, count)]
        if d in DIAGONAL:
            at = CZ - 1 if cz > 0 else 0
            line = CY - 1 if cy > 0 else 0
            j = DIAGONAL.index(d)
            yz_ref[j : j + 1, :] = still[i, at, line : line + 1, :]
        copy = pltpu.make_async_copy(source, new_hbm.at[d, pl.ds(first, count)], sem.at[i])
        copy.start()
        copies.append(copy)
    zp_ref[ZP.index(5)] = still[STILL.index(5), CZ - 1]
    zm_ref[ZM.index(6)] = still[STILL.index(6), 0]
    for copy in copies:
        copy.wait()


def spread(d, plane_of, res, edge, faces):
    _, cy, cz = lattice_velocity[d]
    for z in range(CZ):
        if faces is None and not 0 <= z + cz < CZ:
            continue
        value = plane_of(z)
        if cy > 0:
            if faces is not None:
                faces[0][z, YP.index(d) : YP.index(d) + 1, :] = value[CY - 1 : CY]
            value = pltpu.roll(value, 1, 0)
        elif cy < 0:
            if faces is not None:
                faces[1][z, YM.index(d) : YM.index(d) + 1, :] = value[0:1]
            value = pltpu.roll(value, CY - 1, 0)
        if 0 <= z + cz < CZ:
            res[z + cz] = value
            if cy > 0:
                edge[z + cz] = value[:8]
            elif cy < 0:
                edge[z + cz] = value[CY - 8 :]
        elif cz > 0:
            faces[2][ZP.index(d)] = value
        else:
            faces[3][ZM.index(d)] = value


def collide_step(populations, head):
    return pl.pallas_call(
        collide_body,
        out_shape=(
            shape((19, CZ, CY, CX)),
            near((10, CZ, CY, CX)),
            near((8, ROWS)),
            near((8, ROWS)),
            near((CZ, 8, CX)),
            near((CZ, 8, CX)),
            near((5, CY, CX)),
            near((5, CY, CX)),
            near((6, CZ, 8, CX)),
            near((8, CX)),
        ),
        in_specs=[ANY, VMEM],
        out_specs=(ANY,) + (VMEM,) * 9,
        scratch_shapes=[
            pltpu.VMEM((19, CZ - HEAD, CY, CX), jnp.float32),
            pltpu.VMEM((ROWS, 128), jnp.float32),
            pltpu.VMEM((9, CZ, CY, CX), jnp.float32),
            pltpu.VMEM((9, CZ, CY, CX), jnp.float32),
            pltpu.SemaphoreType.DMA((9,)),
            pltpu.SemaphoreType.DMA((CZ,)),
        ],
        cost_estimate=cost(10_000_000, 5_000_000),
        compiler_params=pltpu.CompilerParams(vmem_limit_bytes=16 * 1024 * 1024),
        name="collide",
    )(far(populations), held(head))


def patched(rel, cols, j, z, first, count):
    cx = lattice_velocity[MOVING[j]][0]
    side, i, at = (0, j, 0) if cx > 0 else (1, j - 5, CX - 1)
    lane = lax.broadcasted_iota(jnp.int32, (count, CX), 1)
    start = z * CY + first
    column = jnp.broadcast_to(cols[side, start : start + count, i : i + 1], (count, CX))
    return jnp.where(lane == at, column, rel[j, z, first : first + count, :])


def faces_body(
    rel, lo_ref, hi_ref, yp_in, ym_in, zp_in, zm_in, yp_ref, ym_ref, zp_ref, zm_ref, cols
):
    yp_ref[...] = yp_in[...]
    ym_ref[...] = ym_in[...]
    zp_ref[...] = zp_in[...]
    zm_ref[...] = zm_in[...]
    pad = jnp.zeros((120, 128), jnp.float32)
    for h in range(2):
        for side, ref in enumerate((lo_ref, hi_ref)):
            block = jnp.concatenate([ref[:, h * 128 : h * 128 + 128], pad], axis=0)
            cols[side, h * 128 : h * 128 + 128, :] = block.T
    for j, d in enumerate(MOVING):
        _, cy, cz = lattice_velocity[d]
        if cz > 0:
            zp_ref[ZP.index(d)] = patched(rel, cols, j, CZ - 1, 0, CY)
        elif cz < 0:
            zm_ref[ZM.index(d)] = patched(rel, cols, j, 0, 0, CY)
        for z in range(CZ):
            if cy > 0:
                i = YP.index(d)
                yp_ref[z, i : i + 1, :] = patched(rel, cols, j, z, CY - 8, 8)[7:8]
            elif cy < 0:
                i = YM.index(d)
                ym_ref[z, i : i + 1, :] = patched(rel, cols, j, z, 0, 8)[0:1]


def faces_step(moving, below, above, faces):
    return pl.pallas_call(
        faces_body,
        out_shape=(
            near((CZ, 8, CX)),
            near((CZ, 8, CX)),
            near((5, CY, CX)),
            near((5, CY, CX)),
            near((2, ROWS, 128)),
        ),
        in_specs=[VMEM] * 7,
        out_specs=(VMEM,) * 5,
        cost_estimate=cost(1_000_000, 500_000),
        compiler_params=pltpu.CompilerParams(vmem_limit_bytes=16 * 1024 * 1024),
        name="faces",
    )(held(moving), held(below), held(above), *[held(f) for f in faces])


def bulk_body(
    new_in,
    w_hbm,
    rel,
    cols,
    place_ref,
    in_ref,
    new_hbm,
    edge_ref,
    out_ref,
    w,
    nodes,
    res,
    sem,
    w_sem,
):
    parts = 8
    w_copies = []
    for c in range(parts):
        blocks = pl.ds(c * (NB // parts), NB // parts)
        w_copies.append(pltpu.make_async_copy(w_hbm.at[blocks], w.at[blocks], w_sem.at[c]))
    for copy in w_copies:
        copy.start()
    copies = []
    for j, d in enumerate(MOVING):
        _, cy, cz = lattice_velocity[d]
        edge = edge_ref.at[BENT.index(d)] if cy != 0 else None
        spread(d, lambda z: patched(rel, cols, j, z, 0, CY), res.at[j], edge, None)
        first, count = (1, CZ - 1) if cz > 0 else (0, CZ - 1) if cz < 0 else (0, CZ)
        planes = pl.ds(first, count)
        copy = pltpu.make_async_copy(res.at[j, planes], new_hbm.at[d, planes], sem.at[j])
        copy.start()
        copies.append(copy)
    place = place_ref[...].astype(jnp.bfloat16)
    for k in range(3):
        arrived = jnp.concatenate(
            [in_ref[pl.ds(3 * r + k, OWNERS, stride=BACK_ROWS), :] for r in range(2)], axis=0
        )
        nodes[pl.ds(k, NB, stride=8), :] = jnp.dot(
            place, arrived.astype(jnp.bfloat16), preferred_element_type=jnp.float32
        )
    for b in range(NB):
        if b % (NB // parts) == 0:
            w_copies[b // (NB // parts)].wait()
        motion = lax.dot_general(
            nodes[b * 8 : b * 8 + 8, :].astype(jnp.bfloat16),
            w[b],
            (((1,), (1,)), ((), ())),
            preferred_element_type=jnp.float32,
        )
        out_ref[:, b, :] = motion[:3]
    for copy in copies:
        copy.wait()


def bulk_step(new, weights, moving, cols, place, arrived):
    return pl.pallas_call(
        bulk_body,
        out_shape=(shape((19, CZ, CY, CX)), near((4, CZ, 8, CX)), shape((3, NB, CX))),
        in_specs=[ANY] * 2 + [VMEM] * 4,
        out_specs=(ANY, VMEM, VMEM),
        input_output_aliases={0: 0},
        scratch_shapes=[
            pltpu.VMEM((NB, CX, SN), jnp.bfloat16),
            pltpu.VMEM((NB * 8, SN), jnp.float32),
            pltpu.VMEM((10, CZ, CY, CX), jnp.float32),
            pltpu.SemaphoreType.DMA((10,)),
            pltpu.SemaphoreType.DMA((8,)),
        ],
        cost_estimate=cost(30_000_000, 5_000_000),
        compiler_params=pltpu.CompilerParams(vmem_limit_bytes=16 * 1024 * 1024),
        name="bulk",
    )(new, far(weights), held(moving), held(cols), held(place), held(arrived))


def finish_body(
    new_in, still_ref, moving_ref, ylo, yhi, zlo, zhi, back_ref, new_hbm, tiles, planes, sem
):
    b, e = lax.axis_index("gy"), lax.axis_index("gz")
    copies = []

    def send(source, target):
        copy = pltpu.make_async_copy(source, target, sem.at[len(copies)])
        copy.start()
        copies.append(copy)

    for sign, dirs, halo, at in ((1, ZP, zlo, 0), (-1, ZM, zhi, CZ - 1)):
        for j, d in enumerate(dirs):
            if d in DIAGONAL:
                cy = lattice_velocity[d][1]
                chunk = lax.rem(b - cy + 4, 4) * 16 + lax.rem(e - sign + 16, 16)
                slot = DIAGONAL.index(d)
                line = 0 if cy > 0 else CY - 1
                planes[slot] = halo[j]
                planes[slot, line : line + 1, :] = back_ref[pl.ds(chunk * BACK_ROWS + 6, 1), :]
                send(planes.at[slot], new_hbm.at[d, at])
            else:
                send(halo.at[j], new_hbm.at[d, at])
    for j, d in enumerate(YP + YM):
        cx, cy, cz = lattice_velocity[d]
        ref, i, at = (ylo, j, 0) if cy > 0 else (yhi, j - 5, CY - 1)
        edge = still_ref.at[TURNED.index(d)] if cx == 0 else moving_ref.at[BENT.index(d)]
        for z in range(CZ):
            if 0 <= z + cz < CZ:
                tiles[j, z + cz] = edge[z + cz]
                tiles[j, z + cz, at % 8 : at % 8 + 1, :] = ref[z, i : i + 1, :]
        first, count = (1, CZ - 1) if cz > 0 else (0, CZ - 1) if cz < 0 else (0, CZ)
        inside = pl.ds(first, count)
        send(tiles.at[j, inside], new_hbm.at[d, inside, pl.ds(at // 8 * 8, 8)])
    for copy in copies:
        copy.wait()


def finish_step(new, still, moving, ylo, yhi, zlo, zhi, back):
    return pl.pallas_call(
        finish_body,
        out_shape=shape((19, CZ, CY, CX)),
        in_specs=[ANY] + [VMEM] * 7,
        out_specs=ANY,
        input_output_aliases={0: 0},
        scratch_shapes=[
            pltpu.VMEM((10, CZ, 8, CX), jnp.float32),
            pltpu.VMEM((4, CY, CX), jnp.float32),
            pltpu.SemaphoreType.DMA((20,)),
        ],
        cost_estimate=cost(100_000, 1_000_000),
        compiler_params=pltpu.CompilerParams(vmem_limit_bytes=16 * 1024 * 1024),
        name="finish",
    )(new, *[held(x) for x in (still, moving, ylo, yhi, zlo, zhi, back)])


def from_behind(value, axis, steps):
    count = lax.axis_size(axis)
    pairs = [(source, (source + steps) % count) for source in range(count)]
    return lax.ppermute(value, axis, pairs)


def exchange(value):
    return lax.all_to_all(value, ("gy", "gz"), split_axis=0, concat_axis=0, tiled=True)


def body(
    populations, rbf_weights, owner_map, shell_slot, compliance, neighbour_compliance, interface_row
):
    owners = owner_map.reshape(1, NB)
    slots = shell_slot.reshape(1, NB)
    outgoing, head, place = send_forces(
        interface_row, owners, slots, populations.reshape(19, ROWS, CX), rbf_weights
    )
    incoming = exchange(outgoing.reshape(OWNERS, 1, OUT_ROWS * 128))
    new, relaxed, xp, xm, yp, ym, zp, zm, still, lines = collide_step(populations, head)
    xlo = from_behind(xp, "gx", 1)
    xhi = from_behind(xm, "gx", -1)
    displacement, back = owner_step(
        incoming.reshape(OWNERS * OUT_ROWS, 128), compliance, neighbour_compliance, lines
    )
    arrived = exchange(back.reshape(OWNERS, 1, BACK_ROWS * 128))
    yp, ym, zp, zm, cols = faces_step(relaxed, xlo, xhi, (yp, ym, zp, zm))
    ylo = from_behind(yp, "gy", 1)
    yhi = from_behind(ym, "gy", -1)
    zlo = from_behind(zp, "gz", 1)
    zhi = from_behind(zm, "gz", -1)
    arrived = arrived.reshape(OWNERS * BACK_ROWS, 128)
    new, bent, wall_motion = bulk_step(new, rbf_weights, relaxed, cols, place, arrived)
    new = finish_step(new, still, bent, ylo, yhi, zlo, zhi, arrived)
    return (new, displacement.transpose(1, 0, 2), wall_motion.transpose(1, 0, 2))


def solution(mesh):
    return jax.shard_map(
        body,
        mesh=mesh,
        in_specs=(
            P(None, "gz", "gy", "gx"),
            P(("gx", "gy", "gz"), None, None),
            P(("gx", "gy", "gz"), None),
            P(("gx", "gy", "gz"), None),
            P(("gx", "gy", "gz"), None, None),
            P(("gx", "gy", "gz"), None),
            P(("gx", "gy", "gz")),
        ),
        out_specs=(
            P(None, "gz", "gy", "gx"),
            P(("gx", "gy", "gz"), None, None),
            P(("gx", "gy", "gz"), None, None),
        ),
        check_vma=False,
    )
```

```python
import jax
import jax.numpy as jnp
from jax import lax
from jax.experimental import pallas as pl
from jax.experimental.pallas import tpu as pltpu
from jax.sharding import PartitionSpec as P


lattice_velocity = (
    (0, 0, 0),
    (1, 0, 0),
    (-1, 0, 0),
    (0, 1, 0),
    (0, -1, 0),
    (0, 0, 1),
    (0, 0, -1),
    (1, 1, 0),
    (-1, -1, 0),
    (1, -1, 0),
    (-1, 1, 0),
    (1, 0, 1),
    (-1, 0, -1),
    (1, 0, -1),
    (-1, 0, 1),
    (0, 1, 1),
    (0, -1, -1),
    (0, 1, -1),
    (0, -1, 1),
)
lattice_weight = (1.0 / 3.0,) + (1.0 / 18.0,) * 6 + (1.0 / 36.0,) * 12
load_scale = 30.0
relaxation = 1.6

CZ, CY, CX = 8, 32, 128
ROWS = CZ * CY
NB, SB, SN = 64, 8, 128
OWNERS = 64
NEAR_BLOCKS = 48
WALL_PIECES = 1
HEAD = 2
OUT_ROWS = 10
BACK_ROWS = 7

VMEM = pl.BlockSpec(memory_space=pltpu.VMEM)
SMEM = pl.BlockSpec(memory_space=pltpu.SMEM)
ANY = pl.BlockSpec(memory_space=pl.ANY)


def moved(component, sign):
    return [d for d in range(19) if lattice_velocity[d][component] == sign]


XP, XM = moved(0, 1), moved(0, -1)
YP, YM = moved(1, 1), moved(1, -1)
ZP, ZM = moved(2, 1), moved(2, -1)
MOVING = XP + XM
PAIRS = list(range(1, 19, 2))
STILL = moved(0, 0)
TURNED = [d for d in STILL if lattice_velocity[d][1] != 0]
BENT = [d for d in MOVING if lattice_velocity[d][1] != 0]
DIAGONAL = [d for d in TURNED if lattice_velocity[d][2] != 0]


def signed_sum(values, component):
    total = None
    for d in values:
        c = lattice_velocity[d][component]
        if c == 0:
            continue
        if total is None:
            total = values[d]
        elif c > 0:
            total = total + values[d]
        else:
            total = total - values[d]
    return total


def signed_total(v, c):
    total = None
    for k in range(3):
        if c[k] != 0:
            term = v[k] if c[k] > 0 else -v[k]
            total = term if total is None else total + term
    return total


def shape(dims, dtype=jnp.float32):
    return jax.ShapeDtypeStruct(dims, dtype)


def near(dims):
    return pltpu.VMEM(dims, jnp.float32)


def held(value):
    return pltpu.with_memory_space_constraint(value, pltpu.VMEM)


def far(value):
    return pltpu.with_memory_space_constraint(value, pltpu.HBM)


def cost(flops, moved_bytes):
    return pl.CostEstimate(flops=flops, bytes_accessed=moved_bytes, transcendentals=0)


def forces_body(
    row_hbm,
    owner_hbm,
    slot_hbm,
    pop_hbm,
    w_hbm,
    out_ref,
    head,
    place_ref,
    row_s,
    owner_v,
    slot_v,
    pop,
    w,
    mom,
    made,
    pop_sem,
    w_sem,
    in_sem,
):
    integers = [
        pltpu.make_async_copy(a, b, in_sem.at[i])
        for i, (a, b) in enumerate(((owner_hbm, owner_v), (slot_hbm, slot_v), (row_hbm, row_s)))
    ]
    rest = pl.ds(HEAD * CY, ROWS - HEAD * CY)
    pop_copies = [
        pltpu.make_async_copy(pop_hbm.at[:, pl.ds(0, HEAD * CY)], head, pop_sem.at[0]),
        pltpu.make_async_copy(pop_hbm.at[:, rest], pop, pop_sem.at[1]),
    ]
    w_copies = []
    pieces = 2
    for c in range(pieces):
        blocks = pl.ds(c * (NB // pieces), NB // pieces)
        w_copies.append(pltpu.make_async_copy(w_hbm.at[blocks], w.at[blocks], w_sem.at[c]))
    for copy in integers + pop_copies + w_copies:
        copy.start()
    for copy in integers:
        copy.wait()

    def iota(dims, axis):
        return lax.broadcasted_iota(jnp.int32, dims, axis).astype(jnp.float32)

    def number(flags):
        return jnp.where(flags, 1.0, 0.0)

    square = (NB, NB)
    owner = owner_v[...].astype(jnp.float32)
    slot = slot_v[...].astype(jnp.float32)
    across = jnp.broadcast_to(owner, square)
    diagonal = iota(square, 0) == iota(square, 1)
    owner_down = jnp.sum(jnp.where(diagonal, across, 0.0), axis=1, keepdims=True)
    same = jnp.broadcast_to(owner_down, square) == across
    rank = jnp.sum(number(same & (iota(square, 0) < iota(square, 1))), axis=0, keepdims=True)
    rank_down = jnp.sum(
        number(same & (iota(square, 1) < iota(square, 0))), axis=1, keepdims=True
    )
    target = jnp.broadcast_to(owner + OWNERS * rank, (2 * OWNERS, NB))
    place = number(target == iota((2 * OWNERS, NB), 0))
    target_down = jnp.broadcast_to(owner_down + OWNERS * rank_down, (NB, 2 * OWNERS))
    place_ref[...] = number(target_down == iota((NB, 2 * OWNERS), 1))
    last = jnp.broadcast_to(slot, square) == SB - 1
    shared = number((across + 1.0 == iota(square, 0)) & last)
    left = jnp.concatenate([place, shared], axis=0).astype(jnp.bfloat16)
    tags = jnp.sum(place * (jnp.broadcast_to(slot, (2 * OWNERS, NB)) + 1.0), axis=1, keepdims=True)
    lane = lax.broadcasted_iota(jnp.int32, (OWNERS, 128), 1)
    first = jnp.broadcast_to(tags[:OWNERS], (OWNERS, 128))
    second = jnp.broadcast_to(tags[OWNERS:], (OWNERS, 128))
    out_ref[pl.ds(9, OWNERS, stride=OUT_ROWS), :] = jnp.where(
        lane == 0, first, jnp.where(lane == 1, second, 0.0)
    )

    for t in range(ROWS // 8):
        if t == 0:
            pop_copies[0].wait()
        elif t == HEAD * CY // 8:
            pop_copies[1].wait()
        ref, at = (head, t * 8) if t < HEAD * CY // 8 else (pop, t * 8 - HEAD * CY)
        values = [ref[d, at : at + 8, :] for d in range(19)]
        gaps = {d: values[d] - values[d + 1] for d in PAIRS}
        for k in range(3):
            mom[pl.ds(t * 64 + k, 8, stride=8), :] = load_scale * signed_sum(gaps, k)
    for b in range(NB):
        if b % (NB // pieces) == 0:
            w_copies[b // (NB // pieces)].wait()
        traction = mom[pl.ds(pl.multiple_of(row_s[b] * 8, 8), 8), :].astype(jnp.bfloat16)
        made[b * 8 : b * 8 + 8, :] = jnp.dot(traction, w[b], preferred_element_type=jnp.float32)
    for k in range(3):
        high, low = two_parts(made[pl.ds(k, NB, stride=8), :])
        rows = jnp.dot(left, high, preferred_element_type=jnp.float32)
        rows = rows + jnp.dot(left, low, preferred_element_type=jnp.float32)
        for g in range(3):
            out_ref[pl.ds(3 * g + k, OWNERS, stride=OUT_ROWS), :] = rows[
                g * OWNERS : (g + 1) * OWNERS
            ]


def send_forces(rows, owners, slots, populations, weights):
    return pl.pallas_call(
        forces_body,
        out_shape=(
            near((OWNERS * OUT_ROWS, 128)),
            near((19, HEAD * CY, CX)),
            near((NB, 2 * OWNERS)),
        ),
        in_specs=[ANY] * 5,
        out_specs=(VMEM, VMEM, VMEM),
        scratch_shapes=[
            pltpu.SMEM((NB,), jnp.int32),
            pltpu.VMEM((1, NB), jnp.int32),
            pltpu.VMEM((1, NB), jnp.int32),
            pltpu.VMEM((19, ROWS - HEAD * CY, CX), jnp.float32),
            pltpu.VMEM((NB, CX, SN), jnp.bfloat16),
            pltpu.VMEM((ROWS * 8, CX), jnp.float32),
            pltpu.VMEM((NB * 8, SN), jnp.float32),
            pltpu.SemaphoreType.DMA((2,)),
            pltpu.SemaphoreType.DMA((2,)),
            pltpu.SemaphoreType.DMA((3,)),
        ],
        cost_estimate=cost(50_000_000, 5_000_000),
        compiler_params=pltpu.CompilerParams(vmem_limit_bytes=16 * 1024 * 1024),
        name="forces",
    )(far(rows), far(owners), far(slots), far(populations), far(weights))


def two_parts(x):
    high = x.astype(jnp.bfloat16)
    return high, (x - high.astype(jnp.float32)).astype(jnp.bfloat16)


def owner_body(in_ref, comp_ref, near_ref, yz_ref, disp_ref, back_ref, left, right):

    b, e = lax.axis_index("gy"), lax.axis_index("gz")
    for j, d in enumerate(DIAGONAL):
        _, cy, cz = lattice_velocity[d]
        chunk = lax.rem(b + cy + 4, 4) * 16 + lax.rem(e + cz + 16, 16)
        back_ref[pl.ds(chunk * BACK_ROWS + 6, 1), :] = yz_ref[j : j + 1, :]

    def rows_of(j):
        return in_ref[pl.ds(j, OWNERS, stride=OUT_ROWS), :]

    def mm(a, b):
        return jnp.dot(a, b, preferred_element_type=jnp.float32)

    tags = rows_of(9)
    lane = lax.broadcasted_iota(jnp.int32, (OWNERS, 128), 1).astype(jnp.float32) + 1.0
    chosen = jnp.concatenate(
        [
            (jnp.broadcast_to(tags[:, r : r + 1], (OWNERS, 128)) == lane).astype(jnp.float32)
            for r in range(2)
        ],
        axis=0,
    )
    select = chosen.T[:SB].astype(jnp.bfloat16)
    left[...] = jnp.zeros(left.shape, jnp.float32)
    for k in range(3):
        arrived = jnp.concatenate([rows_of(k), rows_of(3 + k)], axis=0)
        high, low = two_parts(arrived)
        loads = mm(select, high) + mm(select, low)
        high, low = two_parts(loads)
        left[pl.ds(k, SB, stride=8), :] = high.astype(jnp.float32)
        left[pl.ds(3 + k, SB, stride=8), :] = low.astype(jnp.float32)
        shared = jnp.sum(rows_of(6 + k), axis=0, keepdims=True)
        high, low = two_parts(shared)
        left[SB * 8 + k : SB * 8 + k + 1, :] = high.astype(jnp.float32)
        left[SB * 8 + 3 + k : SB * 8 + 4 + k, :] = low.astype(jnp.float32)

    def product(s, matrix):
        high, low = two_parts(matrix)
        rows = left[s * 8 : s * 8 + 8, :].astype(jnp.bfloat16)
        first = mm(rows, high)
        return first[:3] + first[3:6] + mm(rows, low)[:3]

    for s in range(SB):
        moved_by = product(s, comp_ref[s])
        if s == 0:
            moved_by = moved_by + product(SB, near_ref[...])
        disp_ref[:, s, :] = moved_by
        right[s * 8 : s * 8 + 3, :] = moved_by
    chosen = chosen.astype(jnp.bfloat16)
    for k in range(3):
        nodes = right[pl.ds(k, SB, stride=8), :].astype(jnp.bfloat16).astype(jnp.float32)
        nodes = jnp.concatenate([nodes, jnp.zeros((128 - SB, 128), jnp.float32)], axis=0)
        back = mm(chosen, nodes.astype(jnp.bfloat16))
        for r in range(2):
            back_ref[pl.ds(3 * r + k, OWNERS, stride=BACK_ROWS), :] = back[
                r * OWNERS : (r + 1) * OWNERS
            ]


def owner_step(arrived, compliance, neighbour, lines):
    return pl.pallas_call(
        owner_body,
        out_shape=(shape((3, SB, SN)), near((OWNERS * BACK_ROWS, 128))),
        in_specs=[VMEM] * 4,
        out_specs=(VMEM, VMEM),
        scratch_shapes=[
            pltpu.VMEM((SB * 8 + 8, 128), jnp.float32),
            pltpu.VMEM((SB * 8, 128), jnp.float32),
        ],
        cost_estimate=cost(20_000_000, 1_200_000),
        compiler_params=pltpu.CompilerParams(vmem_limit_bytes=16 * 1024 * 1024),
        name="owner",
    )(held(arrived), held(compliance), held(neighbour), held(lines))


def collide_body(
    pop_hbm,
    head,
    new_hbm,
    rel_ref,
    xp_ref,
    xm_ref,
    yp_ref,
    ym_ref,
    zp_ref,
    zm_ref,
    edge_ref,
    yz_ref,
    pop,
    packed,
    still,
    turned_to,
    sem,
    pop_sem,
):
    arriving = {}
    for first, count in ((HEAD, 2), (HEAD + 2, CZ - HEAD - 2)):
        arriving[first] = pltpu.make_async_copy(
            pop_hbm.at[:, pl.ds(first, count)],
            pop.at[:, pl.ds(first - HEAD, count)],
            pop_sem.at[len(arriving)],
        )
    for copy in arriving.values():
        copy.start()
    lane = lax.broadcasted_iota(jnp.int32, (8, 128), 1)
    for z in range(CZ):
        if z in arriving:
            arriving[z].wait()
        for t in range(CY // 8):
            rows = pl.ds(t * 8, 8)
            if z < HEAD:
                f = [head[d, z * CY + t * 8 : z * CY + t * 8 + 8, :] for d in range(19)]
            else:
                f = [pop[d, z - HEAD, rows, :] for d in range(19)]
            sums = {d: f[d] + f[d + 1] for d in PAIRS}
            gaps = {d: f[d] - f[d + 1] for d in PAIRS}
            density = f[0]
            for d in PAIRS:
                density = density + sums[d]
            inverse = 1.0 / density
            v = [signed_sum(gaps, k) * inverse for k in range(3)]
            speed_square = v[0] * v[0] + v[1] * v[1] + v[2] * v[2]
            base = 1.0 - 1.5 * speed_square
            share = {w: (relaxation * w) * density for w in set(lattice_weight)}
            steady = {w: share[w] * base for w in set(lattice_weight)}
            slope = {w: (3.0 * relaxation * w) * density for w in set(lattice_weight)}
            values = {0: (1.0 - relaxation) * f[0] + steady[lattice_weight[0]]}
            for d in PAIRS:
                w = lattice_weight[d]
                projected = signed_total(v, lattice_velocity[d])
                odd = slope[w] * projected
                even = steady[w] + 1.5 * (odd * projected)
                values[d] = (1.0 - relaxation) * f[d] + (even + odd)
                values[d + 1] = (1.0 - relaxation) * f[d + 1] + (even - odd)
            pack = jnp.zeros((8, 128), jnp.float32)
            for d in range(19):
                c = lattice_velocity[d]
                value = values[d]
                if c[0] > 0:
                    i = XP.index(d)
                    value = pltpu.roll(value, 1, 1)
                    edge = value if i == 0 else pltpu.roll(value, i, 1)
                    pack = jnp.where(lane == i, edge, pack)
                elif c[0] < 0:
                    i = 8 + XM.index(d)
                    value = pltpu.roll(value, 127, 1)
                    pack = jnp.where(lane == i, pltpu.roll(value, i + 1, 1), pack)
                if c[0] != 0:
                    rel_ref[MOVING.index(d), z, rows, :] = value
                else:
                    still[STILL.index(d), z, rows, :] = value
            packed[pl.ds(z * CY + t * 8, 8), :] = pack

    for h in range(2):
        turned = packed[h * 128 : h * 128 + 128, :].T
        xp_ref[:, h * 128 : h * 128 + 128] = turned[0:8]
        xm_ref[:, h * 128 : h * 128 + 128] = turned[8:16]

    copies = []
    for i, d in enumerate(STILL):
        _, cy, cz = lattice_velocity[d]
        first, count = (1, CZ - 1) if cz > 0 else (0, CZ - 1) if cz < 0 else (0, CZ)
        if cy == 0:
            source = still.at[i, pl.ds(first - cz, count)]
        else:
            faces = (yp_ref, ym_ref, zp_ref, zm_ref)
            spread(d, lambda z: still[i, z], turned_to.at[i], edge_ref.at[TURNED.index(d)], faces)
            source = turned_to.at[i, pl.ds(first, count)]
        if d in DIAGONAL:
            at = CZ - 1 if cz > 0 else 0
            line = CY - 1 if cy > 0 else 0
            j = DIAGONAL.index(d)
            yz_ref[j : j + 1, :] = still[i, at, line : line + 1, :]
        copy = pltpu.make_async_copy(source, new_hbm.at[d, pl.ds(first, count)], sem.at[i])
        copy.start()
        copies.append(copy)
    zp_ref[ZP.index(5)] = still[STILL.index(5), CZ - 1]
    zm_ref[ZM.index(6)] = still[STILL.index(6), 0]
    for copy in copies:
        copy.wait()


def spread(d, plane_of, res, edge, faces):
    _, cy, cz = lattice_velocity[d]
    for z in range(CZ):
        if faces is None and not 0 <= z + cz < CZ:
            continue
        value = plane_of(z)
        if cy > 0:
            if faces is not None:
                faces[0][z, YP.index(d) : YP.index(d) + 1, :] = value[CY - 1 : CY]
            value = pltpu.roll(value, 1, 0)
        elif cy < 0:
            if faces is not None:
                faces[1][z, YM.index(d) : YM.index(d) + 1, :] = value[0:1]
            value = pltpu.roll(value, CY - 1, 0)
        if 0 <= z + cz < CZ:
            res[z + cz] = value
            if cy > 0:
                edge[z + cz] = value[:8]
            elif cy < 0:
                edge[z + cz] = value[CY - 8 :]
        elif cz > 0:
            faces[2][ZP.index(d)] = value
        else:
            faces[3][ZM.index(d)] = value


def collide_step(populations, head):
    return pl.pallas_call(
        collide_body,
        out_shape=(
            shape((19, CZ, CY, CX)),
            near((10, CZ, CY, CX)),
            near((8, ROWS)),
            near((8, ROWS)),
            near((CZ, 8, CX)),
            near((CZ, 8, CX)),
            near((5, CY, CX)),
            near((5, CY, CX)),
            near((6, CZ, 8, CX)),
            near((8, CX)),
        ),
        in_specs=[ANY, VMEM],
        out_specs=(ANY,) + (VMEM,) * 9,
        scratch_shapes=[
            pltpu.VMEM((19, CZ - HEAD, CY, CX), jnp.float32),
            pltpu.VMEM((ROWS, 128), jnp.float32),
            pltpu.VMEM((9, CZ, CY, CX), jnp.float32),
            pltpu.VMEM((9, CZ, CY, CX), jnp.float32),
            pltpu.SemaphoreType.DMA((9,)),
            pltpu.SemaphoreType.DMA((2,)),
        ],
        cost_estimate=cost(10_000_000, 5_000_000),
        compiler_params=pltpu.CompilerParams(vmem_limit_bytes=16 * 1024 * 1024),
        name="collide",
    )(far(populations), held(head))


def patched(rel, cols, j, z, first, count):
    cx = lattice_velocity[MOVING[j]][0]
    side, i, at = (0, j, 0) if cx > 0 else (1, j - 5, CX - 1)
    lane = lax.broadcasted_iota(jnp.int32, (count, CX), 1)
    start = z * CY + first
    column = jnp.broadcast_to(cols[side, start : start + count, i : i + 1], (count, CX))
    return jnp.where(lane == at, column, rel[j, z, first : first + count, :])


def faces_body(
    rel, lo_ref, hi_ref, yp_in, ym_in, zp_in, zm_in, yp_ref, ym_ref, zp_ref, zm_ref, cols
):
    yp_ref[...] = yp_in[...]
    ym_ref[...] = ym_in[...]
    zp_ref[...] = zp_in[...]
    zm_ref[...] = zm_in[...]
    pad = jnp.zeros((120, 128), jnp.float32)
    for h in range(2):
        for side, ref in enumerate((lo_ref, hi_ref)):
            block = jnp.concatenate([ref[:, h * 128 : h * 128 + 128], pad], axis=0)
            cols[side, h * 128 : h * 128 + 128, :] = block.T
    for j, d in enumerate(MOVING):
        _, cy, cz = lattice_velocity[d]
        if cz > 0:
            zp_ref[ZP.index(d)] = patched(rel, cols, j, CZ - 1, 0, CY)
        elif cz < 0:
            zm_ref[ZM.index(d)] = patched(rel, cols, j, 0, 0, CY)
        for z in range(CZ):
            if cy > 0:
                i = YP.index(d)
                yp_ref[z, i : i + 1, :] = patched(rel, cols, j, z, CY - 8, 8)[7:8]
            elif cy < 0:
                i = YM.index(d)
                ym_ref[z, i : i + 1, :] = patched(rel, cols, j, z, 0, 8)[0:1]


def faces_step(moving, below, above, faces):
    return pl.pallas_call(
        faces_body,
        out_shape=(
            near((CZ, 8, CX)),
            near((CZ, 8, CX)),
            near((5, CY, CX)),
            near((5, CY, CX)),
            near((2, ROWS, 128)),
        ),
        in_specs=[VMEM] * 7,
        out_specs=(VMEM,) * 5,
        cost_estimate=cost(1_000_000, 500_000),
        compiler_params=pltpu.CompilerParams(vmem_limit_bytes=16 * 1024 * 1024),
        name="faces",
    )(held(moving), held(below), held(above), *[held(f) for f in faces])


def stream_body(new_in, w_hbm, rel, cols, new_hbm, edge_ref, w_ref, res, sem, w_sem):
    w_copy = pltpu.make_async_copy(w_hbm.at[pl.ds(0, NEAR_BLOCKS)], w_ref, w_sem)
    w_copy.start()
    copies = []
    for j, d in enumerate(MOVING):
        _, cy, cz = lattice_velocity[d]
        edge = edge_ref.at[BENT.index(d)] if cy != 0 else None
        spread(d, lambda z: patched(rel, cols, j, z, 0, CY), res.at[j], edge, None)
        first, count = (1, CZ - 1) if cz > 0 else (0, CZ - 1) if cz < 0 else (0, CZ)
        planes = pl.ds(first, count)
        copy = pltpu.make_async_copy(res.at[j, planes], new_hbm.at[d, planes], sem.at[j])
        copy.start()
        copies.append(copy)
    w_copy.wait()
    for copy in copies:
        copy.wait()


def stream_step(new, weights, moving, cols):
    return pl.pallas_call(
        stream_body,
        out_shape=(
            shape((19, CZ, CY, CX)),
            near((4, CZ, 8, CX)),
            pltpu.VMEM((NEAR_BLOCKS, CX, SN), jnp.bfloat16),
        ),
        in_specs=[ANY] * 2 + [VMEM] * 2,
        out_specs=(ANY, VMEM, VMEM),
        input_output_aliases={0: 0},
        scratch_shapes=[
            pltpu.VMEM((10, CZ, CY, CX), jnp.float32),
            pltpu.SemaphoreType.DMA((10,)),
            pltpu.SemaphoreType.DMA,
        ],
        cost_estimate=cost(10_000_000, 4_000_000),
        compiler_params=pltpu.CompilerParams(vmem_limit_bytes=16 * 1024 * 1024),
        name="stream",
    )(new, far(weights), held(moving), held(cols))


def wall_body(place_ref, in_ref, w_near, w_hbm, out_ref, w, nodes, w_sem):
    w_copies = []
    for c in range(WALL_PIECES):
        size = (NB - NEAR_BLOCKS) // WALL_PIECES
        w_copies.append(
            pltpu.make_async_copy(
                w_hbm.at[pl.ds(NEAR_BLOCKS + c * size, size)], w.at[pl.ds(c * size, size)], w_sem.at[c]
            )
        )
    for copy in w_copies:
        copy.start()
    place = place_ref[...].astype(jnp.bfloat16)
    for k in range(3):
        arrived = jnp.concatenate(
            [in_ref[pl.ds(3 * r + k, OWNERS, stride=BACK_ROWS), :] for r in range(2)], axis=0
        )
        nodes[pl.ds(k, NB, stride=8), :] = jnp.dot(
            place, arrived.astype(jnp.bfloat16), preferred_element_type=jnp.float32
        )
    for b in range(NB):
        if b < NEAR_BLOCKS:
            weight = w_near[b]
        else:
            if (b - NEAR_BLOCKS) % size == 0:
                w_copies[(b - NEAR_BLOCKS) // size].wait()
            weight = w[b - NEAR_BLOCKS]
        motion = lax.dot_general(
            nodes[b * 8 : b * 8 + 8, :].astype(jnp.bfloat16),
            weight,
            (((1,), (1,)), ((), ())),
            preferred_element_type=jnp.float32,
        )
        out_ref[:, b, :] = motion[:3]


def wall_step(place, arrived, first_weights, weights):
    return pl.pallas_call(
        wall_body,
        out_shape=shape((3, NB, CX)),
        in_specs=[VMEM, VMEM, VMEM, ANY],
        out_specs=VMEM,
        scratch_shapes=[
            pltpu.VMEM((NB - NEAR_BLOCKS, CX, SN), jnp.bfloat16),
            pltpu.VMEM((NB * 8, SN), jnp.float32),
            pltpu.SemaphoreType.DMA((WALL_PIECES,)),
        ],
        cost_estimate=cost(20_000_000, 2_500_000),
        compiler_params=pltpu.CompilerParams(vmem_limit_bytes=16 * 1024 * 1024),
        name="wall",
    )(held(place), held(arrived), held(first_weights), far(weights))


def finish_body(
    new_in, still_ref, moving_ref, ylo, yhi, zlo, zhi, back_ref, new_hbm, tiles, planes, sem
):
    b, e = lax.axis_index("gy"), lax.axis_index("gz")
    copies = []

    def send(source, target):
        copy = pltpu.make_async_copy(source, target, sem.at[len(copies)])
        copy.start()
        copies.append(copy)

    for sign, dirs, halo, at in ((1, ZP, zlo, 0), (-1, ZM, zhi, CZ - 1)):
        for j, d in enumerate(dirs):
            if d in DIAGONAL:
                cy = lattice_velocity[d][1]
                chunk = lax.rem(b - cy + 4, 4) * 16 + lax.rem(e - sign + 16, 16)
                slot = DIAGONAL.index(d)
                line = 0 if cy > 0 else CY - 1
                planes[slot] = halo[j]
                planes[slot, line : line + 1, :] = back_ref[pl.ds(chunk * BACK_ROWS + 6, 1), :]
                send(planes.at[slot], new_hbm.at[d, at])
            else:
                send(halo.at[j], new_hbm.at[d, at])
    for j, d in enumerate(YP + YM):
        cx, cy, cz = lattice_velocity[d]
        ref, i, at = (ylo, j, 0) if cy > 0 else (yhi, j - 5, CY - 1)
        edge = still_ref.at[TURNED.index(d)] if cx == 0 else moving_ref.at[BENT.index(d)]
        for z in range(CZ):
            if 0 <= z + cz < CZ:
                tiles[j, z + cz] = edge[z + cz]
                tiles[j, z + cz, at % 8 : at % 8 + 1, :] = ref[z, i : i + 1, :]
        first, count = (1, CZ - 1) if cz > 0 else (0, CZ - 1) if cz < 0 else (0, CZ)
        inside = pl.ds(first, count)
        send(tiles.at[j, inside], new_hbm.at[d, inside, pl.ds(at // 8 * 8, 8)])
    for copy in copies:
        copy.wait()


def finish_step(new, still, moving, ylo, yhi, zlo, zhi, back):
    return pl.pallas_call(
        finish_body,
        out_shape=shape((19, CZ, CY, CX)),
        in_specs=[ANY] + [VMEM] * 7,
        out_specs=ANY,
        input_output_aliases={0: 0},
        scratch_shapes=[
            pltpu.VMEM((10, CZ, 8, CX), jnp.float32),
            pltpu.VMEM((4, CY, CX), jnp.float32),
            pltpu.SemaphoreType.DMA((20,)),
        ],
        cost_estimate=cost(100_000, 1_000_000),
        compiler_params=pltpu.CompilerParams(vmem_limit_bytes=16 * 1024 * 1024),
        name="finish",
    )(new, *[held(x) for x in (still, moving, ylo, yhi, zlo, zhi, back)])


def from_behind(value, axis, steps):
    count = lax.axis_size(axis)
    pairs = [(source, (source + steps) % count) for source in range(count)]
    return lax.ppermute(value, axis, pairs)


def exchange(value):
    return lax.all_to_all(value, ("gy", "gz"), split_axis=0, concat_axis=0, tiled=True)


def body(
    populations, rbf_weights, owner_map, shell_slot, compliance, neighbour_compliance, interface_row
):
    owners = owner_map.reshape(1, NB)
    slots = shell_slot.reshape(1, NB)
    outgoing, head, place = send_forces(
        interface_row, owners, slots, populations.reshape(19, ROWS, CX), rbf_weights
    )
    incoming = exchange(outgoing.reshape(OWNERS, 1, OUT_ROWS * 128))
    new, relaxed, xp, xm, yp, ym, zp, zm, still, lines = collide_step(populations, head)
    xlo = from_behind(xp, "gx", 1)
    xhi = from_behind(xm, "gx", -1)
    displacement, back = owner_step(
        incoming.reshape(OWNERS * OUT_ROWS, 128), compliance, neighbour_compliance, lines
    )
    arrived = exchange(back.reshape(OWNERS, 1, BACK_ROWS * 128))
    yp, ym, zp, zm, cols = faces_step(relaxed, xlo, xhi, (yp, ym, zp, zm))
    ylo = from_behind(yp, "gy", 1)
    yhi = from_behind(ym, "gy", -1)
    zlo = from_behind(zp, "gz", 1)
    zhi = from_behind(zm, "gz", -1)
    arrived = arrived.reshape(OWNERS * BACK_ROWS, 128)
    new, bent, weights = stream_step(new, rbf_weights, relaxed, cols)
    wall_motion = wall_step(place, arrived, weights, rbf_weights)
    new = finish_step(new, still, bent, ylo, yhi, zlo, zhi, arrived)
    return (new, displacement.transpose(1, 0, 2), wall_motion.transpose(1, 0, 2))


def solution(mesh):
    return jax.shard_map(
        body,
        mesh=mesh,
        in_specs=(
            P(None, "gz", "gy", "gx"),
            P(("gx", "gy", "gz"), None, None),
            P(("gx", "gy", "gz"), None),
            P(("gx", "gy", "gz"), None),
            P(("gx", "gy", "gz"), None, None),
            P(("gx", "gy", "gz"), None),
            P(("gx", "gy", "gz")),
        ),
        out_specs=(
            P(None, "gz", "gy", "gx"),
            P(("gx", "gy", "gz"), None, None),
            P(("gx", "gy", "gz"), None, None),
        ),
        check_vma=False,
    )
```
